256 devices in a mesh: seq: 16 (over z, core), grp: 16 (over x, y).
Axes of the slice: x: 4, y: 4, z: 8, core: 2. Of those that a mesh axis runs over, the one named last changes fastest.
Arguments:
- tokens: bfloat16 [131072, 1536], P(('seq', 'grp')), may hold values from -6 to 6
- w_query: bfloat16 [1536, 768], replicated, may hold values from -0.15625 to 0.15625
- w_key: bfloat16 [1536, 768], replicated, may hold values from -0.15625 to 0.15625
- w_value: bfloat16 [1536, 768], replicated, may hold values from -0.15625 to 0.15625
- w_output: bfloat16 [768, 1536], replicated, may hold values from -0.21875 to 0.21875
- level_weights: float32 [9, 6], replicated, may hold values from 0.05 to 0.5
Outputs:
- mixed: bfloat16 [131072, 1536], P(('seq', 'grp'))
The draws below stay inside these ranges and needn't reach their ends.
All inputs are finite; a program needn't handle non-finite values.
Results may differ from the reference program's by a relative error of at most 0.013.
Values may be sent and summed in bfloat16 or wider, within the bound.
No kernel may reach another device: no remote copies, remote signals or barrier semaphores. Data moves between devices by JAX's collectives and lax.ppermute only.
A program may use at most 128 MiB of HBM per device.

```python
import math
import jax
import jax.numpy as jnp
from jax import lax

D = 1536
HEADS = 6
HEAD_DIM = 128
LEVELS = 9
TOK_DEV = 512
INNER = 768
TOKENS = 131072
N_SEQ = 16
N_GRP = 16


def level_of(rng, shape, pieces, low, high):
    level = 1.0
    for position, shards_of in pieces:
        steps = jax.random.uniform(jax.random.fold_in(jax.random.fold_in(rng, 6), position), (shards_of,), jnp.float32, low / len(pieces), high / len(pieces))
        level = level * jnp.repeat(jnp.exp(steps), shape[position] // shards_of).reshape((-1,) + (1,) * (len(shape) - 1 - position))
    return level


def scatter_about(key, extent, deviation, limit, pieces=(), kind=jnp.bfloat16):
    entries = jax.random.normal(key, extent, jnp.float32) * deviation
    if len(pieces) > 0:
        entries = level_of(key, extent, pieces, -0.22, 0.18) * entries
    return jnp.clip(entries, min=-limit, max=limit).astype(kind)


def setup_inputs(seed: int = 0) -> dict:
    key_list = jax.random.split(jax.random.key(seed), 7)
    tokens = scatter_about(key_list[0], (TOKENS, D), 1.0, 6.0, ((0, 256),))
    w_query = scatter_about(key_list[1], (D, INNER), D ** -0.5, 0.15625)
    w_key = scatter_about(key_list[2], (D, INNER), D ** -0.5, 0.15625)
    w_value = scatter_about(key_list[3], (D, INNER), D ** -0.5, 0.15625)
    w_output = scatter_about(key_list[4], (INNER, D), INNER ** -0.5, 0.21875)
    level_weights = jnp.clip(jnp.exp(jax.random.uniform(key_list[5], (LEVELS, HEADS), jnp.float32, math.log(0.05), math.log(0.5))), 0.05, 0.5)
    return {"tokens": tokens, "w_query": w_query, "w_key": w_key, "w_value": w_value, "w_output": w_output, "level_weights": level_weights}


def unit_heads(matrix):
    return (matrix * lax.rsqrt(lax.optimization_barrier(jnp.sum(matrix * matrix, -1, keepdims=True)) + 1e-06)).astype(jnp.bfloat16)

def reference(tokens, w_query, w_key, w_value, w_output, level_weights):
    blocks = N_SEQ * N_GRP
    query = unit_heads(jnp.dot(tokens, w_query, preferred_element_type=jnp.float32).reshape(TOKENS, HEADS, HEAD_DIM))
    keys = unit_heads(jnp.dot(tokens, w_key, preferred_element_type=jnp.float32).reshape(TOKENS, HEADS, HEAD_DIM))
    values = jnp.dot(tokens, w_value, preferred_element_type=jnp.float32).astype(jnp.bfloat16).reshape(TOKENS, HEADS, HEAD_DIM)
    query_blocks = query.reshape(blocks, TOK_DEV, HEADS, HEAD_DIM)
    key_blocks = keys.reshape(blocks, TOK_DEV, HEADS, HEAD_DIM)
    value_blocks = values.reshape(blocks, TOK_DEV, HEADS, HEAD_DIM)
    states = jnp.einsum('prhd,prhe->phde', key_blocks.astype(jnp.float32), value_blocks.astype(jnp.float32))
    positions = jnp.arange(blocks, dtype=jnp.int32)
    combined = jnp.zeros((blocks, HEADS, HEAD_DIM, HEAD_DIM), jnp.float32)
    for level in range(blocks.bit_length() - 1):
        grouped = states.reshape(blocks >> level, 1 << level, HEADS, HEAD_DIM, HEAD_DIM).sum(1)
        sibling = jnp.maximum((positions >> level) - 1, 0).astype(jnp.int32)
        present = (positions >> level & 1).astype(jnp.float32)
        factor = level_weights[level + 1] * 2.0 ** (-0.5 * level)
        combined = combined + present[:, None, None, None] * factor[None, :, None, None] * grouped[sibling]
    combined = combined.astype(jnp.bfloat16)
    causal = jnp.arange(TOK_DEV)[:, None] >= jnp.arange(TOK_DEV)[None, :]

    def one_block(operands):
        block_query, block_keys, block_values, block_state = operands
        query32 = block_query.astype(jnp.float32)
        scores = jnp.einsum('thd,shd->hts', query32, block_keys.astype(jnp.float32))
        weights = (jnp.where(causal[None], scores, 0.0) * level_weights[0][:, None, None]).astype(jnp.bfloat16)
        inside = jnp.einsum('hts,she->the', weights.astype(jnp.float32), block_values.astype(jnp.float32))
        earlier = jnp.einsum('thd,hde->the', query32, block_state.astype(jnp.float32))
        return (inside + earlier).astype(jnp.bfloat16)
    attended = lax.map(one_block, (query_blocks, key_blocks, value_blocks, combined))
    attended = attended.reshape(TOKENS, INNER)
    return jnp.dot(attended, w_output, preferred_element_type=jnp.float32).astype(jnp.bfloat16)
```

```python
import functools

import jax
import jax.numpy as jnp
from jax import lax
from jax.experimental import pallas as pl
from jax.experimental.pallas import tpu as pltpu
from jax.sharding import PartitionSpec as P

BF16 = jnp.bfloat16
F32 = jnp.float32
VMEM = pl.BlockSpec(memory_space=pltpu.VMEM)
SMEM = pl.BlockSpec(memory_space=pltpu.SMEM)
ANY = pl.BlockSpec(memory_space=pl.ANY)
HBM = pl.BlockSpec(memory_space=pltpu.HBM)
QUARTERS = 4


def unit(matrix):
    return (matrix * lax.rsqrt(jnp.sum(matrix * matrix, -1, keepdims=True) + 1e-06)).astype(BF16)


def unit_pair(matrix, width):
    return jnp.concatenate([unit(matrix[:, :width]), unit(matrix[:, width:])], 1)


def dot(a, b):
    return jnp.dot(a, b, preferred_element_type=F32)


def state_kernel(
    width,
    tok_hbm,
    wk_hbm,
    wv_hbm,
    wq_hbm,
    k_ref,
    v_ref,
    tok,
    wq,
    own,
    one,
    two,
    three,
    wk,
    wv,
    slices,
    sems,
):
    depth = tok.shape[1]
    pair = 2 * width
    pairs = wk.shape[0]
    half = depth // 2
    part = width // QUARTERS
    parts = [
        pltpu.make_async_copy(
            tok_hbm.at[:, pl.ds(i * half, half)], tok.at[:, pl.ds(i * half, half)], sems.at[i]
        )
        for i in range(2)
    ]
    weights = []
    for j in range(pairs):
        for source, target in ((wk_hbm, wk), (wv_hbm, wv)):
            weights.append(
                pltpu.make_async_copy(
                    source.at[:, pl.ds(j * pair, pair)], target.at[j], sems.at[2 + len(weights)]
                )
            )
    last = pltpu.make_async_copy(wq_hbm, wq, sems.at[2 + 2 * pairs])
    parts[0].start()
    weights[0].start()
    parts[1].start()
    for copy in weights[1:]:
        copy.start()
    last.start()
    parts[0].wait()
    weights[0].wait()
    for j in range(pairs):
        if j == 0:
            k32 = dot(tok[:, :half], wk[j, :half])
            parts[1].wait()
            k32 = k32 + dot(tok[:, half:], wk[j, half:])
        else:
            weights[2 * j].wait()
            k32 = dot(tok[...], wk[j])
        keys = unit_pair(k32, width)
        k_ref[:, j * pair : (j + 1) * pair] = keys
        weights[2 * j + 1].wait()
        values = dot(tok[...], wv[j]).astype(BF16)
        v_ref[:, j * pair : (j + 1) * pair] = values
        both = lax.dot_general(keys, values, (((0,), (0,)), ((), ())), preferred_element_type=F32)
        for side in range(2):
            head = 2 * j + side
            state = both[side * width : (side + 1) * width, side * width : (side + 1) * width]
            for q in range(QUARTERS):
                slices[q, head * part : (head + 1) * part, :] = state[
                    q * part : (q + 1) * part
                ].astype(BF16)
    y = lax.axis_index("grp") % QUARTERS
    for distance, target in enumerate((own, one, two, three)):
        target[...] = slices[y ^ distance]
    last.wait()


def states_of(tokens, w_key, w_value, w_query, heads, width):
    rows, depth = tokens.shape
    inner = heads * width
    pairs = heads // 2
    piece = jax.ShapeDtypeStruct((inner // QUARTERS, width), BF16)
    side = jax.ShapeDtypeStruct((rows, inner), BF16)
    whole = [jax.ShapeDtypeStruct(a.shape, a.dtype) for a in (tokens, w_query)]
    return pl.pallas_call(
        functools.partial(state_kernel, width),
        out_shape=(side, side, *whole, piece, piece, piece, piece),
        in_specs=[HBM] * 4,
        out_specs=[VMEM] * 8,
        scratch_shapes=[
            pltpu.VMEM((pairs, depth, 2 * width), BF16),
            pltpu.VMEM((pairs, depth, 2 * width), BF16),
            pltpu.VMEM((QUARTERS, inner // QUARTERS, width), BF16),
            pltpu.SemaphoreType.DMA((3 + 2 * pairs,)),
        ],
        compiler_params=pltpu.CompilerParams(vmem_limit_bytes=20 << 20),
        name="states",
    )(*(pltpu.with_memory_space_constraint(a, pltpu.HBM) for a in (tokens, w_key, w_value, w_query)))


def query_kernel(width, tok, wq, q_ref):
    pair = 2 * width
    for j in range(wq.shape[1] // pair):
        columns = slice(j * pair, (j + 1) * pair)
        q_ref[:, columns] = unit_pair(dot(tok[...], wq[:, columns]), width)


def query_of(tok, wq, width):
    return pl.pallas_call(
        functools.partial(query_kernel, width),
        out_shape=jax.ShapeDtypeStruct((tok.shape[0], wq.shape[1]), BF16),
        in_specs=[VMEM, VMEM],
        out_specs=VMEM,
        compiler_params=pltpu.CompilerParams(vmem_limit_bytes=12 << 20),
        name="query",
    )(tok, wq)


def inside_kernel(width, first, q_ref, k_ref, v_ref, levels, after, inside_ref):
    rows, columns_here = inside_ref.shape
    block = rows // 2
    low = lax.broadcasted_iota(jnp.int32, (block, block), 0) >= lax.broadcasted_iota(
        jnp.int32, (block, block), 1
    )
    for local in range(columns_here // width):
        head = first + local
        columns = slice(head * width, (head + 1) * width)
        scale = levels[0, head]
        for i in range(2):
            here = slice(i * block, (i + 1) * block)
            q = q_ref[here, columns]

            def weigh(keys, masked):
                scores = lax.dot_general(
                    q, keys, (((1,), (1,)), ((), ())), preferred_element_type=F32
                )
                if masked:
                    scores = jnp.where(low, scores, 0.0)
                return (scores * scale).astype(BF16)

            out = dot(weigh(k_ref[here, columns], True), v_ref[here, columns])
            if i:
                out = out + dot(weigh(k_ref[:block, columns], False), v_ref[:block, columns])
            inside_ref[here, local * width : (local + 1) * width] = out


def inside_of(query, keys, values, level_weights, after, first, count, width):
    return pl.pallas_call(
        functools.partial(inside_kernel, width, first),
        out_shape=jax.ShapeDtypeStruct((query.shape[0], count * width), F32),
        in_specs=[VMEM, VMEM, VMEM, SMEM, ANY],
        out_specs=VMEM,
        compiler_params=pltpu.CompilerParams(vmem_limit_bytes=12 << 20),
        name="inside",
    )(query, keys, values, level_weights, after)


def gather_kernel(levels, *refs):
    near = refs[:4]
    x1, x2, x3, other, z1, z2, z3, local_ref, last_ref = refs[4:]
    member = lax.axis_index("grp")
    group = lax.axis_index("seq")
    y, x, core, z = member % 4, member // 4, group % 2, group // 2
    heads = levels.shape[1]
    part = last_ref.shape[0] // heads

    def bit(index, level):
        return ((index >> level) & 1).astype(F32)

    for head in range(heads):
        rows = slice(head * part, (head + 1) * part)

        def factor(level, present):
            return levels[level + 1, head] * (present * 2.0 ** (-0.5 * level))

        def read(ref):
            return ref[rows, :].astype(F32)

        far = (
            factor(2, bit(x, 0)) * read(x1)
            + factor(3, bit(x, 1)) * (read(x2) + read(x3))
            + factor(4, bit(core, 0)) * read(other)
            + factor(5, bit(z, 0)) * read(z1)
            + factor(6, bit(z, 1)) * (read(z2) + read(z3))
        )
        sides = [read(ref) for ref in near]
        for distance in range(4):
            target = y ^ distance
            local_ref[distance, rows, :] = (
                far
                + factor(0, bit(target, 0)) * sides[distance ^ 1]
                + factor(1, bit(target, 1)) * (sides[distance ^ 2] + sides[distance ^ 3])
            )
        last_ref[rows, :] = jnp.full(
            (part, last_ref.shape[1]), factor(7, bit(z, 2)), F32
        )


def gather_of(level_weights, near, others):
    shape = near[0].shape
    return pl.pallas_call(
        gather_kernel,
        out_shape=(
            jax.ShapeDtypeStruct((4, *shape), F32),
            jax.ShapeDtypeStruct(shape, F32),
        ),
        in_specs=[SMEM] + [VMEM] * 11,
        out_specs=[VMEM, VMEM],
        compiler_params=pltpu.CompilerParams(vmem_limit_bytes=4 << 20),
        name="gather",
    )(level_weights, *near, *others)


def mix_kernel(
    width, q_ref, low_ref, high_ref, own, one, two, three, wo, out_hbm, slices, attended, out, sems
):
    rows, inner = q_ref.shape
    part = width // QUARTERS
    pair = 2 * width
    y = lax.axis_index("grp") % QUARTERS
    for distance, source in enumerate((own, one, two, three)):
        slices[y ^ distance] = source[...]
    half = inner // 2
    zero = jnp.zeros((width, width), BF16)
    for j in range(inner // pair):
        halves = []
        insides = []
        for side in range(2):
            head = 2 * j + side
            state = jnp.concatenate(
                [slices[q, head * part : (head + 1) * part, :] for q in range(QUARTERS)], 0
            )
            halves.append(jnp.concatenate([zero, state] if side else [state, zero], 1))
            start = head * width
            insides.append(
                low_ref[:, start : start + width]
                if start < half
                else high_ref[:, start - half : start - half + width]
            )
        columns = slice(j * pair, (j + 1) * pair)
        earlier = dot(q_ref[:, columns], jnp.concatenate(halves, 0))
        attended[:, columns] = (jnp.concatenate(insides, 1) + earlier).astype(BF16)
    steps = sems.shape[0]
    block = out.shape[1] // steps
    copies = []
    for i in range(steps):
        columns = pl.ds(i * block, block)
        out[:, columns] = dot(attended[...], wo[:, columns]).astype(BF16)
        copy = pltpu.make_async_copy(out.at[:, columns], out_hbm.at[:, columns], sems.at[i])
        copy.start()
        copies.append(copy)
    for copy in copies:
        copy.wait()


def mixed_of(query, insides, pieces, w_output, width):
    rows, inner = query.shape
    wide = w_output.shape[1]
    return pl.pallas_call(
        functools.partial(mix_kernel, width),
        out_shape=jax.ShapeDtypeStruct((rows, wide), BF16),
        in_specs=[VMEM] * 8,
        out_specs=HBM,
        scratch_shapes=[
            pltpu.VMEM((QUARTERS, inner // QUARTERS, width), BF16),
            pltpu.VMEM((rows, inner), BF16),
            pltpu.VMEM((rows, wide), BF16),
            pltpu.SemaphoreType.DMA((6,)),
        ],
        compiler_params=pltpu.CompilerParams(vmem_limit_bytes=16 << 20),
        name="mix",
    )(query, *insides, *pieces, w_output)


def flip(value, axis, mask):
    pairs = [(source, source ^ mask) for source in range(lax.axis_size(axis))]
    return lax.ppermute(value, axis, pairs)


def flips(value, axis, masks):
    return [flip(value, axis, mask) for mask in masks]


def plus(total, others):
    for other in others:
        total = total + other.astype(F32)
    return total


def per_device(tokens, w_query, w_key, w_value, w_output, level_weights):
    heads = level_weights.shape[1]
    width = w_query.shape[1] // heads
    keys, values, tok, wq, *sent = states_of(tokens, w_key, w_value, w_query, heads, width)
    near = [sent[0]] + [None] * 3
    for distance in (3, 1, 2):
        near[distance] = flip(sent[distance], "grp", distance)
    query = query_of(tok, wq, width)
    *near, query = lax.optimization_barrier((*near, query))
    total = plus(near[0].astype(F32), near[1:])

    going = total.astype(BF16)
    x3, x1, x2 = flips(going, "grp", (12, 4, 8))
    low = inside_of(query, keys, values, level_weights, going, 0, heads // 2, width)
    x3, x1, x2, low = lax.optimization_barrier((x3, x1, x2, low))
    total = plus(total, (x1, x2, x3))
    (other,) = flips(total.astype(BF16), "seq", (1,))
    total = plus(total, (other,))
    going = total.astype(BF16)
    z1, z2, z3 = flips(going, "seq", (2, 4, 6))
    high = inside_of(query, keys, values, level_weights, going, heads // 2, heads // 2, width)
    z1, z2, z3, high = lax.optimization_barrier((z1, z2, z3, high))
    total = plus(total, (z1, z2, z3))
    (past,) = flips(total.astype(BF16), "seq", (12,))
    gathered, factor = gather_of(level_weights, near, (x1, x2, x3, other, z1, z2, z3))
    past, gathered, factor = lax.optimization_barrier((past, gathered, factor))
    back = [
        (gathered[distance] + factor * past.astype(F32)).astype(BF16) for distance in range(4)
    ]
    pieces = [back[0]] + [None] * 3
    for distance in (3, 1, 2):
        pieces[distance] = flip(back[distance], "grp", distance)
    return mixed_of(query, (low, high), pieces, w_output, width)


def solution(mesh):
    placed = (P(("seq", "grp"), None), P(), P(), P(), P(), P())
    return jax.shard_map(
        per_device, mesh=mesh, in_specs=placed, out_specs=P(("seq", "grp"), None), check_vma=False
    )
```

```python
import functools

import jax
import jax.numpy as jnp
from jax import lax
from jax.experimental import pallas as pl
from jax.experimental.pallas import tpu as pltpu
from jax.sharding import PartitionSpec as P

BF16 = jnp.bfloat16
F32 = jnp.float32
VMEM = pl.BlockSpec(memory_space=pltpu.VMEM)
SMEM = pl.BlockSpec(memory_space=pltpu.SMEM)
ANY = pl.BlockSpec(memory_space=pl.ANY)
HBM = pl.BlockSpec(memory_space=pltpu.HBM)
QUARTERS = 4


def unit(matrix):
    return (matrix * lax.rsqrt(jnp.sum(matrix * matrix, -1, keepdims=True) + 1e-06)).astype(BF16)


def unit_pair(matrix, width):
    return jnp.concatenate([unit(matrix[:, :width]), unit(matrix[:, width:])], 1)


def dot(a, b):
    return jnp.dot(a, b, preferred_element_type=F32)


def state_kernel(
    width,
    tok_hbm,
    wk_hbm,
    wv_hbm,
    wq_hbm,
    k_ref,
    v_ref,
    tok,
    wq,
    own,
    one,
    two,
    three,
    wk,
    wv,
    slices,
    sems,
):
    depth = tok.shape[1]
    pair = 2 * width
    pairs = wk.shape[0]
    half = depth // 2
    part = width // QUARTERS
    parts = [
        pltpu.make_async_copy(
            tok_hbm.at[:, pl.ds(i * half, half)], tok.at[:, pl.ds(i * half, half)], sems.at[i]
        )
        for i in range(2)
    ]
    weights = []
    for j in range(pairs):
        for source, target in ((wk_hbm, wk), (wv_hbm, wv)):
            weights.append(
                pltpu.make_async_copy(
                    source.at[:, pl.ds(j * pair, pair)], target.at[j], sems.at[2 + len(weights)]
                )
            )
    last = pltpu.make_async_copy(wq_hbm, wq, sems.at[2 + 2 * pairs])
    parts[0].start()
    weights[0].start()
    parts[1].start()
    for copy in weights[1:]:
        copy.start()
    last.start()
    parts[0].wait()
    weights[0].wait()
    for j in range(pairs):
        if j == 0:
            k32 = dot(tok[:, :half], wk[j, :half])
            parts[1].wait()
            k32 = k32 + dot(tok[:, half:], wk[j, half:])
        else:
            weights[2 * j].wait()
            k32 = dot(tok[...], wk[j])
        keys = unit_pair(k32, width)
        k_ref[:, j * pair : (j + 1) * pair] = keys
        weights[2 * j + 1].wait()
        values = dot(tok[...], wv[j]).astype(BF16)
        v_ref[:, j * pair : (j + 1) * pair] = values
        both = lax.dot_general(keys, values, (((0,), (0,)), ((), ())), preferred_element_type=F32)
        for side in range(2):
            head = 2 * j + side
            state = both[side * width : (side + 1) * width, side * width : (side + 1) * width]
            for q in range(QUARTERS):
                slices[q, head * part : (head + 1) * part, :] = state[
                    q * part : (q + 1) * part
                ].astype(BF16)
    y = lax.axis_index("grp") % QUARTERS
    for distance, target in enumerate((own, one, two, three)):
        target[...] = slices[y ^ distance]
    last.wait()


def states_of(tokens, w_key, w_value, w_query, heads, width):
    rows, depth = tokens.shape
    inner = heads * width
    pairs = heads // 2
    piece = jax.ShapeDtypeStruct((inner // QUARTERS, width), BF16)
    side = jax.ShapeDtypeStruct((rows, inner), BF16)
    whole = [jax.ShapeDtypeStruct(a.shape, a.dtype) for a in (tokens, w_query)]
    return pl.pallas_call(
        functools.partial(state_kernel, width),
        out_shape=(side, side, *whole, piece, piece, piece, piece),
        in_specs=[HBM] * 4,
        out_specs=[VMEM] * 8,
        scratch_shapes=[
            pltpu.VMEM((pairs, depth, 2 * width), BF16),
            pltpu.VMEM((pairs, depth, 2 * width), BF16),
            pltpu.VMEM((QUARTERS, inner // QUARTERS, width), BF16),
            pltpu.SemaphoreType.DMA((3 + 2 * pairs,)),
        ],
        compiler_params=pltpu.CompilerParams(vmem_limit_bytes=20 << 20),
        name="states",
    )(*(pltpu.with_memory_space_constraint(a, pltpu.HBM) for a in (tokens, w_key, w_value, w_query)))


def query_kernel(width, tok, wq, q_ref):
    pair = 2 * width
    for j in range(wq.shape[1] // pair):
        columns = slice(j * pair, (j + 1) * pair)
        q_ref[:, columns] = unit_pair(dot(tok[...], wq[:, columns]), width)


def query_of(tok, wq, width):
    return pl.pallas_call(
        functools.partial(query_kernel, width),
        out_shape=jax.ShapeDtypeStruct((tok.shape[0], wq.shape[1]), BF16),
        in_specs=[VMEM, VMEM],
        out_specs=VMEM,
        compiler_params=pltpu.CompilerParams(vmem_limit_bytes=12 << 20),
        name="query",
    )(tok, wq)


def inside_kernel(width, first, q_ref, k_ref, v_ref, levels, after, inside_ref):
    rows, columns_here = inside_ref.shape
    block = rows // 2
    low = lax.broadcasted_iota(jnp.int32, (block, block), 0) >= lax.broadcasted_iota(
        jnp.int32, (block, block), 1
    )
    for local in range(columns_here // width):
        head = first + local
        columns = slice(head * width, (head + 1) * width)
        scale = levels[0, head]
        for i in range(2):
            here = slice(i * block, (i + 1) * block)
            q = q_ref[here, columns]

            def weigh(keys, masked):
                scores = lax.dot_general(
                    q, keys, (((1,), (1,)), ((), ())), preferred_element_type=F32
                )
                if masked:
                    scores = jnp.where(low, scores, 0.0)
                return (scores * scale).astype(BF16)

            out = dot(weigh(k_ref[here, columns], True), v_ref[here, columns])
            if i:
                out = out + dot(weigh(k_ref[:block, columns], False), v_ref[:block, columns])
            inside_ref[here, local * width : (local + 1) * width] = out


def inside_of(query, keys, values, level_weights, after, first, count, width):
    return pl.pallas_call(
        functools.partial(inside_kernel, width, first),
        out_shape=jax.ShapeDtypeStruct((query.shape[0], count * width), F32),
        in_specs=[VMEM, VMEM, VMEM, SMEM, ANY],
        out_specs=VMEM,
        compiler_params=pltpu.CompilerParams(vmem_limit_bytes=12 << 20),
        name="inside",
    )(query, keys, values, level_weights, after)


def gather_kernel(levels, *refs):
    near = refs[:4]
    x1, x2, x3, other, z1, z2, z3, local_ref, last_ref = refs[4:]
    member = lax.axis_index("grp")
    group = lax.axis_index("seq")
    y, x, core, z = member % 4, member // 4, group % 2, group // 2
    heads = levels.shape[1]
    part = last_ref.shape[0] // heads

    def bit(index, level):
        return ((index >> level) & 1).astype(F32)

    for head in range(heads):
        rows = slice(head * part, (head + 1) * part)

        def factor(level, present):
            return levels[level + 1, head] * (present * 2.0 ** (-0.5 * level))

        def read(ref):
            return ref[rows, :].astype(F32)

        far = (
            factor(2, bit(x, 0)) * read(x1)
            + factor(3, bit(x, 1)) * (read(x2) + read(x3))
            + factor(4, bit(core, 0)) * read(other)
            + factor(5, bit(z, 0)) * read(z1)
            + factor(6, bit(z, 1)) * (read(z2) + read(z3))
        )
        sides = [read(ref) for ref in near]
        for distance in range(4):
            target = y ^ distance
            local_ref[distance, rows, :] = (
                far
                + factor(0, bit(target, 0)) * sides[distance ^ 1]
                + factor(1, bit(target, 1)) * (sides[distance ^ 2] + sides[distance ^ 3])
            )
        last_ref[rows, :] = jnp.full(
            (part, last_ref.shape[1]), factor(7, bit(z, 2)), F32
        )


def gather_of(level_weights, near, others):
    shape = near[0].shape
    return pl.pallas_call(
        gather_kernel,
        out_shape=(
            jax.ShapeDtypeStruct((4, *shape), F32),
            jax.ShapeDtypeStruct(shape, F32),
        ),
        in_specs=[SMEM] + [VMEM] * 11,
        out_specs=[VMEM, VMEM],
        compiler_params=pltpu.CompilerParams(vmem_limit_bytes=4 << 20),
        name="gather",
    )(level_weights, *near, *others)


def mix_kernel(
    width, q_ref, low_ref, high_ref, own, one, two, three, wo, out_hbm, slices, attended, out, sems
):
    rows, inner = q_ref.shape
    part = width // QUARTERS
    pair = 2 * width
    y = lax.axis_index("grp") % QUARTERS
    for distance, source in enumerate((own, one, two, three)):
        slices[y ^ distance] = source[...]
    half = inner // 2
    zero = jnp.zeros((width, width), BF16)
    for j in range(inner // pair):
        halves = []
        insides = []
        for side in range(2):
            head = 2 * j + side
            state = jnp.concatenate(
                [slices[q, head * part : (head + 1) * part, :] for q in range(QUARTERS)], 0
            )
            halves.append(jnp.concatenate([zero, state] if side else [state, zero], 1))
            start = head * width
            insides.append(
                low_ref[:, start : start + width]
                if start < half
                else high_ref[:, start - half : start - half + width]
            )
        columns = slice(j * pair, (j + 1) * pair)
        earlier = dot(q_ref[:, columns], jnp.concatenate(halves, 0))
        attended[:, columns] = (jnp.concatenate(insides, 1) + earlier).astype(BF16)
    steps = sems.shape[0]
    block = out.shape[1] // steps
    copies = []
    for i in range(steps):
        columns = pl.ds(i * block, block)
        out[:, columns] = dot(attended[...], wo[:, columns]).astype(BF16)
        copy = pltpu.make_async_copy(out.at[:, columns], out_hbm.at[:, columns], sems.at[i])
        copy.start()
        copies.append(copy)
    for copy in copies:
        copy.wait()


def mixed_of(query, insides, pieces, w_output, width):
    rows, inner = query.shape
    wide = w_output.shape[1]
    return pl.pallas_call(
        functools.partial(mix_kernel, width),
        out_shape=jax.ShapeDtypeStruct((rows, wide), BF16),
        in_specs=[VMEM] * 8,
        out_specs=HBM,
        scratch_shapes=[
            pltpu.VMEM((QUARTERS, inner // QUARTERS, width), BF16),
            pltpu.VMEM((rows, inner), BF16),
            pltpu.VMEM((rows, wide), BF16),
            pltpu.SemaphoreType.DMA((6,)),
        ],
        compiler_params=pltpu.CompilerParams(vmem_limit_bytes=16 << 20),
        name="mix",
    )(query, *insides, *pieces, w_output)


def flip(value, axis, mask):
    pairs = [(source, source ^ mask) for source in range(lax.axis_size(axis))]
    return lax.ppermute(value, axis, pairs)


def flips(value, axis, masks):
    return [flip(value, axis, mask) for mask in masks]


def plus(total, others):
    for other in others:
        total = total + other.astype(F32)
    return total


def per_device(tokens, w_query, w_key, w_value, w_output, level_weights):
    heads = level_weights.shape[1]
    width = w_query.shape[1] // heads
    keys, values, tok, wq, *sent = states_of(tokens, w_key, w_value, w_query, heads, width)
    near = [sent[0]] + [None] * 3
    for distance in (2, 1, 3):
        near[distance] = flip(sent[distance], "grp", distance)
    query = query_of(tok, wq, width)
    near[2], near[1], near[3], near[0], query = lax.optimization_barrier(
        (near[2], near[1], near[3], near[0], query)
    )
    total = plus(near[0].astype(F32), near[1:])

    going = total.astype(BF16)
    x2, x1, x3 = flips(going, "grp", (8, 4, 12))
    low = inside_of(query, keys, values, level_weights, going, 0, heads // 2, width)
    x2, x1, x3, low = lax.optimization_barrier((x2, x1, x3, low))
    total = plus(total, (x1, x2, x3))
    (other,) = flips(total.astype(BF16), "seq", (1,))
    total = plus(total, (other,))
    going = total.astype(BF16)
    z3, z2, z1 = flips(going, "seq", (6, 4, 2))
    high = inside_of(query, keys, values, level_weights, going, heads // 2, heads // 2, width)
    z3, z2, z1, high = lax.optimization_barrier((z3, z2, z1, high))
    total = plus(total, (z1, z2, z3))
    (past,) = flips(total.astype(BF16), "seq", (12,))
    gathered, factor = gather_of(level_weights, near, (x1, x2, x3, other, z1, z2, z3))
    past, gathered, factor = lax.optimization_barrier((past, gathered, factor))
    back = [
        (gathered[distance] + factor * past.astype(F32)).astype(BF16) for distance in range(4)
    ]
    pieces = [back[0]] + [None] * 3
    for distance in (2, 1, 3):
        pieces[distance] = flip(back[distance], "grp", distance)
    pieces[2], pieces[1], pieces[3], pieces[0] = lax.optimization_barrier(
        (pieces[2], pieces[1], pieces[3], pieces[0])
    )
    return mixed_of(query, (low, high), pieces, w_output, width)


def solution(mesh):
    placed = (P(("seq", "grp"), None), P(), P(), P(), P(), P())
    return jax.shard_map(
        per_device, mesh=mesh, in_specs=placed, out_specs=P(("seq", "grp"), None), check_vma=False
    )
```

```python
import functools

import jax
import jax.numpy as jnp
from jax import lax
from jax.experimental import pallas as pl
from jax.experimental.pallas import tpu as pltpu
from jax.sharding import PartitionSpec as P

BF16 = jnp.bfloat16
F32 = jnp.float32
VMEM = pl.BlockSpec(memory_space=pltpu.VMEM)
SMEM = pl.BlockSpec(memory_space=pltpu.SMEM)
ANY = pl.BlockSpec(memory_space=pl.ANY)
HBM = pl.BlockSpec(memory_space=pltpu.HBM)
QUARTERS = 4


def unit(matrix):
    return (matrix * lax.rsqrt(jnp.sum(matrix * matrix, -1, keepdims=True) + 1e-06)).astype(BF16)


def unit_pair(matrix, width):
    return jnp.concatenate([unit(matrix[:, :width]), unit(matrix[:, width:])], 1)


def dot(a, b):
    return jnp.dot(a, b, preferred_element_type=F32)


def state_kernel(
    width,
    tok_hbm,
    wk_hbm,
    wv_hbm,
    wq_hbm,
    k_ref,
    v_ref,
    tok,
    wq,
    own,
    one,
    two,
    three,
    weights,
    slices,
    sums,
    sems,
):
    depth = tok.shape[1]
    pair = 2 * width
    part = width // QUARTERS
    chunks = 3
    chunk = depth // chunks
    count = 0

    def copy(source, target):
        nonlocal count
        count += 1
        return pltpu.make_async_copy(source, target, sems.at[count - 1])

    def columns(start, size):
        return pl.ds(start * pair, size * pair)

    first = []
    for i in range(chunks):
        rows = pl.ds(i * chunk, chunk)
        first.append(copy(tok_hbm.at[:, rows], tok.at[:, rows]))
        first.append(copy(wk_hbm.at[rows, columns(0, 2)], weights.at[0, rows]))
    second = [
        copy(wk_hbm.at[:, columns(2, 1)], weights.at[1, :, columns(0, 1)]),
        copy(wv_hbm.at[:, columns(0, 1)], weights.at[1, :, columns(1, 1)]),
    ]
    third = copy(wv_hbm.at[:, columns(1, 2)], weights.at[2])
    last = copy(wq_hbm, wq)
    for item in (*first, *second, third, last):
        item.start()

    def finish_keys(j, product):
        k_ref[:, j * pair : (j + 1) * pair] = unit_pair(product, width)

    def finish_values(j, product):
        here = slice(j * pair, (j + 1) * pair)
        values = product.astype(BF16)
        v_ref[:, here] = values
        both = lax.dot_general(
            k_ref[:, here], values, (((0,), (0,)), ((), ())), preferred_element_type=F32
        )
        for side in range(2):
            head = 2 * j + side
            state = both[side * width : (side + 1) * width, side * width : (side + 1) * width]
            for q in range(QUARTERS):
                slices[q, head * part : (head + 1) * part, :] = state[
                    q * part : (q + 1) * part
                ].astype(BF16)

    for i in range(chunks):
        first[2 * i].wait()
        first[2 * i + 1].wait()
        rows = slice(i * chunk, (i + 1) * chunk)
        product = dot(tok[:, rows], weights[0, rows])
        sums[0] = product if i == 0 else sums[0] + product
    for item in second:
        item.wait()
    sums[1] = dot(tok[...], weights[1])
    finish_keys(0, sums[0, :, :pair])
    finish_keys(1, sums[0, :, pair:])
    third.wait()
    sums[0] = dot(tok[...], weights[2])
    finish_keys(2, sums[1, :, :pair])
    finish_values(0, sums[1, :, pair:])
    finish_values(1, sums[0, :, :pair])
    finish_values(2, sums[0, :, pair:])
    y = lax.axis_index("grp") % QUARTERS
    for distance, target in enumerate((own, one, two, three)):
        target[...] = slices[y ^ distance]
    last.wait()


def states_of(tokens, w_key, w_value, w_query, heads, width):
    rows, depth = tokens.shape
    inner = heads * width
    piece = jax.ShapeDtypeStruct((inner // QUARTERS, width), BF16)
    side = jax.ShapeDtypeStruct((rows, inner), BF16)
    whole = [jax.ShapeDtypeStruct(a.shape, a.dtype) for a in (tokens, w_query)]
    operands = (tokens, w_key, w_value, w_query)
    return pl.pallas_call(
        functools.partial(state_kernel, width),
        out_shape=(side, side, *whole, piece, piece, piece, piece),
        in_specs=[HBM] * 4,
        out_specs=[VMEM] * 8,
        scratch_shapes=[
            pltpu.VMEM((3, depth, 4 * width), BF16),
            pltpu.VMEM((QUARTERS, inner // QUARTERS, width), BF16),
            pltpu.VMEM((2, rows, 4 * width), F32),
            pltpu.SemaphoreType.DMA((10,)),
        ],
        compiler_params=pltpu.CompilerParams(vmem_limit_bytes=24 << 20),
        name="states",
    )(*(pltpu.with_memory_space_constraint(operand, pltpu.HBM) for operand in operands))


def query_kernel(width, tok, wq, q_ref):
    pair = 2 * width
    for j in range(wq.shape[1] // pair):
        columns = slice(j * pair, (j + 1) * pair)
        q_ref[:, columns] = unit_pair(dot(tok[...], wq[:, columns]), width)


def query_of(tok, wq, width):
    return pl.pallas_call(
        functools.partial(query_kernel, width),
        out_shape=jax.ShapeDtypeStruct((tok.shape[0], wq.shape[1]), BF16),
        in_specs=[VMEM, VMEM],
        out_specs=VMEM,
        compiler_params=pltpu.CompilerParams(vmem_limit_bytes=12 << 20),
        name="query",
    )(tok, wq)


def inside_kernel(width, first, q_ref, k_ref, v_ref, levels, after, inside_ref):
    rows, columns_here = inside_ref.shape
    block = rows // 2
    low = lax.broadcasted_iota(jnp.int32, (block, block), 0) >= lax.broadcasted_iota(
        jnp.int32, (block, block), 1
    )
    for local in range(columns_here // width):
        head = first + local
        columns = slice(head * width, (head + 1) * width)
        scale = levels[0, head]
        for i in range(2):
            here = slice(i * block, (i + 1) * block)
            q = q_ref[here, columns]

            def weigh(keys, masked):
                scores = lax.dot_general(
                    q, keys, (((1,), (1,)), ((), ())), preferred_element_type=F32
                )
                if masked:
                    scores = jnp.where(low, scores, 0.0)
                return (scores * scale).astype(BF16)

            out = dot(weigh(k_ref[here, columns], True), v_ref[here, columns])
            if i:
                out = out + dot(weigh(k_ref[:block, columns], False), v_ref[:block, columns])
            inside_ref[here, local * width : (local + 1) * width] = out


def inside_of(query, keys, values, level_weights, after, first, count, width):
    return pl.pallas_call(
        functools.partial(inside_kernel, width, first),
        out_shape=jax.ShapeDtypeStruct((query.shape[0], count * width), F32),
        in_specs=[VMEM, VMEM, VMEM, SMEM, ANY],
        out_specs=VMEM,
        compiler_params=pltpu.CompilerParams(vmem_limit_bytes=12 << 20),
        name="inside",
    )(query, keys, values, level_weights, after)


def gather_kernel(levels, *refs):
    near = refs[:4]
    x1, x2, x3, other, z1, z2, z3, local_ref, last_ref = refs[4:]
    member = lax.axis_index("grp")
    group = lax.axis_index("seq")
    y, x, core, z = member % 4, member // 4, group % 2, group // 2
    heads = levels.shape[1]
    part = last_ref.shape[0] // heads

    def bit(index, level):
        return ((index >> level) & 1).astype(F32)

    for head in range(heads):
        rows = slice(head * part, (head + 1) * part)

        def factor(level, present):
            return levels[level + 1, head] * (present * 2.0 ** (-0.5 * level))

        def read(ref):
            return ref[rows, :].astype(F32)

        far = (
            factor(2, bit(x, 0)) * read(x1)
            + factor(3, bit(x, 1)) * (read(x2) + read(x3))
            + factor(4, bit(core, 0)) * read(other)
            + factor(5, bit(z, 0)) * read(z1)
            + factor(6, bit(z, 1)) * (read(z2) + read(z3))
        )
        sides = [read(ref) for ref in near]
        for distance in range(4):
            target = y ^ distance
            local_ref[distance, rows, :] = (
                far
                + factor(0, bit(target, 0)) * sides[distance ^ 1]
                + factor(1, bit(target, 1)) * (sides[distance ^ 2] + sides[distance ^ 3])
            )
        last_ref[rows, :] = jnp.full(
            (part, last_ref.shape[1]), factor(7, bit(z, 2)), F32
        )


def gather_of(level_weights, near, others):
    shape = near[0].shape
    return pl.pallas_call(
        gather_kernel,
        out_shape=(
            jax.ShapeDtypeStruct((4, *shape), F32),
            jax.ShapeDtypeStruct(shape, F32),
        ),
        in_specs=[SMEM] + [VMEM] * 11,
        out_specs=[VMEM, VMEM],
        compiler_params=pltpu.CompilerParams(vmem_limit_bytes=4 << 20),
        name="gather",
    )(level_weights, *near, *others)


def mix_kernel(
    width, q_ref, low_ref, high_ref, own, one, two, three, wo, out_hbm, slices, attended, out, sems
):
    rows, inner = q_ref.shape
    part = width // QUARTERS
    pair = 2 * width
    y = lax.axis_index("grp") % QUARTERS
    for distance, source in enumerate((own, one, two, three)):
        slices[y ^ distance] = source[...]
    half = inner // 2
    zero = jnp.zeros((width, width), BF16)
    for j in range(inner // pair):
        halves = []
        insides = []
        for side in range(2):
            head = 2 * j + side
            state = jnp.concatenate(
                [slices[q, head * part : (head + 1) * part, :] for q in range(QUARTERS)], 0
            )
            halves.append(jnp.concatenate([zero, state] if side else [state, zero], 1))
            start = head * width
            insides.append(
                low_ref[:, start : start + width]
                if start < half
                else high_ref[:, start - half : start - half + width]
            )
        columns = slice(j * pair, (j + 1) * pair)
        earlier = dot(q_ref[:, columns], jnp.concatenate(halves, 0))
        attended[:, columns] = (jnp.concatenate(insides, 1) + earlier).astype(BF16)
    steps = sems.shape[0]
    block = out.shape[1] // steps
    copies = []
    for i in range(steps):
        columns = pl.ds(i * block, block)
        out[:, columns] = dot(attended[...], wo[:, columns]).astype(BF16)
        copy = pltpu.make_async_copy(out.at[:, columns], out_hbm.at[:, columns], sems.at[i])
        copy.start()
        copies.append(copy)
    for copy in copies:
        copy.wait()


def mixed_of(query, insides, pieces, w_output, width):
    rows, inner = query.shape
    wide = w_output.shape[1]
    return pl.pallas_call(
        functools.partial(mix_kernel, width),
        out_shape=jax.ShapeDtypeStruct((rows, wide), BF16),
        in_specs=[VMEM] * 8,
        out_specs=HBM,
        scratch_shapes=[
            pltpu.VMEM((QUARTERS, inner // QUARTERS, width), BF16),
            pltpu.VMEM((rows, inner), BF16),
            pltpu.VMEM((rows, wide), BF16),
            pltpu.SemaphoreType.DMA((6,)),
        ],
        compiler_params=pltpu.CompilerParams(vmem_limit_bytes=16 << 20),
        name="mix",
    )(query, *insides, *pieces, w_output)


def flip(value, axis, mask):
    pairs = [(source, source ^ mask) for source in range(lax.axis_size(axis))]
    return lax.ppermute(value, axis, pairs)


def flips(value, axis, masks):
    return [flip(value, axis, mask) for mask in masks]


def plus(total, others):
    for other in others:
        total = total + other.astype(F32)
    return total


def per_device(tokens, w_query, w_key, w_value, w_output, level_weights):
    heads = level_weights.shape[1]
    width = w_query.shape[1] // heads
    keys, values, tok, wq, *sent = states_of(tokens, w_key, w_value, w_query, heads, width)
    near = [sent[0]] + [None] * 3
    for distance in (2, 1, 3):
        near[distance] = flip(sent[distance], "grp", distance)
    query = query_of(tok, wq, width)
    near[2], near[1], near[3], near[0], query = lax.optimization_barrier(
        (near[2], near[1], near[3], near[0], query)
    )
    total = plus(near[0].astype(F32), near[1:])

    going = total.astype(BF16)
    x2, x1, x3 = flips(going, "grp", (8, 4, 12))
    low = inside_of(query, keys, values, level_weights, going, 0, heads // 2, width)
    x2, x1, x3, low = lax.optimization_barrier((x2, x1, x3, low))
    total = plus(total, (x1, x2, x3))
    (other,) = flips(total.astype(BF16), "seq", (1,))
    total = plus(total, (other,))
    going = total.astype(BF16)
    z3, z2, z1 = flips(going, "seq", (7, 5, 3))
    high = inside_of(query, keys, values, level_weights, going, heads // 2, heads // 2, width)
    z3, z2, z1, high = lax.optimization_barrier((z3, z2, z1, high))
    total = plus(total, (z1, z2, z3))
    (past,) = flips(total.astype(BF16), "seq", (13,))
    gathered, factor = gather_of(level_weights, near, (x1, x2, x3, other, z1, z2, z3))
    past, gathered, factor = lax.optimization_barrier((past, gathered, factor))
    back = [
        (gathered[distance] + factor * past.astype(F32)).astype(BF16) for distance in range(4)
    ]
    pieces = [back[0]] + [None] * 3
    for distance in (2, 1, 3):
        pieces[distance] = flip(back[distance], "grp", distance)
    pieces[2], pieces[1], pieces[3], pieces[0] = lax.optimization_barrier(
        (pieces[2], pieces[1], pieces[3], pieces[0])
    )
    return mixed_of(query, (low, high), pieces, w_output, width)


def solution(mesh):
    placed = (P(("seq", "grp"), None), P(), P(), P(), P(), P())
    return jax.shard_map(
        per_device, mesh=mesh, in_specs=placed, out_specs=P(("seq", "grp"), None), check_vma=False
    )
```

```python
import functools

import jax
import jax.numpy as jnp
from jax import lax
from jax.experimental import pallas as pl
from jax.experimental.pallas import tpu as pltpu
from jax.sharding import PartitionSpec as P

BF16 = jnp.bfloat16
F32 = jnp.float32
VMEM = pl.BlockSpec(memory_space=pltpu.VMEM)
SMEM = pl.BlockSpec(memory_space=pltpu.SMEM)
ANY = pl.BlockSpec(memory_space=pl.ANY)
HBM = pl.BlockSpec(memory_space=pltpu.HBM)
QUARTERS = 4


def unit(matrix):
    return (matrix * lax.rsqrt(jnp.sum(matrix * matrix, -1, keepdims=True) + 1e-06)).astype(BF16)


def unit_pair(matrix, width):
    return jnp.concatenate([unit(matrix[:, :width]), unit(matrix[:, width:])], 1)


def dot(a, b):
    return jnp.dot(a, b, preferred_element_type=F32)


def state_kernel(
    width,
    tok_hbm,
    wk_hbm,
    wv_hbm,
    wq_hbm,
    k_ref,
    v_ref,
    tok,
    wq,
    own,
    one,
    two,
    three,
    weights,
    slices,
    sums,
    sems,
):
    depth = tok.shape[1]
    pair = 2 * width
    part = width // QUARTERS
    chunks = 3
    chunk = depth // chunks
    count = 0

    def copy(source, target):
        nonlocal count
        count += 1
        return pltpu.make_async_copy(source, target, sems.at[count - 1])

    def columns(start, size):
        return pl.ds(start * pair, size * pair)

    first = []
    for i in range(chunks):
        rows = pl.ds(i * chunk, chunk)
        first.append(copy(tok_hbm.at[:, rows], tok.at[:, rows]))
        first.append(copy(wk_hbm.at[rows, columns(0, 2)], weights.at[0, rows]))
    second = [
        copy(wk_hbm.at[:, columns(2, 1)], weights.at[1, :, columns(0, 1)]),
        copy(wv_hbm.at[:, columns(0, 1)], weights.at[1, :, columns(1, 1)]),
    ]
    third = copy(wv_hbm.at[:, columns(1, 2)], weights.at[2])
    last = copy(wq_hbm, wq)
    for item in (*first, *second, third, last):
        item.start()

    def finish_keys(j, product):
        k_ref[:, j * pair : (j + 1) * pair] = unit_pair(product, width)

    def finish_values(j, product):
        here = slice(j * pair, (j + 1) * pair)
        values = product.astype(BF16)
        v_ref[:, here] = values
        both = lax.dot_general(
            k_ref[:, here], values, (((0,), (0,)), ((), ())), preferred_element_type=F32
        )
        for side in range(2):
            head = 2 * j + side
            state = both[side * width : (side + 1) * width, side * width : (side + 1) * width]
            for q in range(QUARTERS):
                slices[q, head * part : (head + 1) * part, :] = state[
                    q * part : (q + 1) * part
                ].astype(BF16)

    for i in range(chunks):
        first[2 * i].wait()
        first[2 * i + 1].wait()
        rows = slice(i * chunk, (i + 1) * chunk)
        product = dot(tok[:, rows], weights[0, rows])
        sums[0] = product if i == 0 else sums[0] + product
    for item in second:
        item.wait()
    sums[1] = dot(tok[...], weights[1])
    finish_keys(0, sums[0, :, :pair])
    finish_keys(1, sums[0, :, pair:])
    third.wait()
    sums[0] = dot(tok[...], weights[2])
    finish_keys(2, sums[1, :, :pair])
    finish_values(0, sums[1, :, pair:])
    finish_values(1, sums[0, :, :pair])
    finish_values(2, sums[0, :, pair:])
    y = lax.axis_index("grp") % QUARTERS
    for distance, target in enumerate((own, one, two, three)):
        target[...] = slices[y ^ distance]
    last.wait()


def states_of(tokens, w_key, w_value, w_query, heads, width):
    rows, depth = tokens.shape
    inner = heads * width
    piece = jax.ShapeDtypeStruct((inner // QUARTERS, width), BF16)
    side = jax.ShapeDtypeStruct((rows, inner), BF16)
    whole = [jax.ShapeDtypeStruct(a.shape, a.dtype) for a in (tokens, w_query)]
    operands = (tokens, w_key, w_value, w_query)
    return pl.pallas_call(
        functools.partial(state_kernel, width),
        out_shape=(side, side, *whole, piece, piece, piece, piece),
        in_specs=[HBM] * 4,
        out_specs=[VMEM] * 8,
        scratch_shapes=[
            pltpu.VMEM((3, depth, 4 * width), BF16),
            pltpu.VMEM((QUARTERS, inner // QUARTERS, width), BF16),
            pltpu.VMEM((2, rows, 4 * width), F32),
            pltpu.SemaphoreType.DMA((10,)),
        ],
        compiler_params=pltpu.CompilerParams(vmem_limit_bytes=24 << 20),
        name="states",
    )(*(pltpu.with_memory_space_constraint(operand, pltpu.HBM) for operand in operands))


def position():
    member = lax.axis_index("grp")
    group = lax.axis_index("seq")
    return member % 4, member // 4, group % 2, group // 2


def bit(index, level):
    return ((index >> level) & 1).astype(F32)


def query_kernel(width, tok, wq, levels, q_ref, factors):
    pair = 2 * width
    for j in range(wq.shape[1] // pair):
        columns = slice(j * pair, (j + 1) * pair)
        q_ref[:, columns] = unit_pair(dot(tok[...], wq[:, columns]), width)
    x, z = position()[1], position()[3]
    heads = levels.shape[1]
    part = factors.shape[1] // heads
    for head in range(heads):
        rows = slice(head * part, (head + 1) * part)
        for slot, (level, present) in enumerate(((2, bit(x, 0)), (3, bit(x, 1)), (7, bit(z, 2)))):
            value = levels[level + 1, head] * (present * 2.0 ** (-0.5 * level))
            factors[slot, rows, :] = jnp.full((part, factors.shape[2]), value, F32)


def query_of(tok, wq, level_weights, width):
    rows, inner = tok.shape[0], wq.shape[1]
    return pl.pallas_call(
        functools.partial(query_kernel, width),
        out_shape=(
            jax.ShapeDtypeStruct((rows, inner), BF16),
            jax.ShapeDtypeStruct((3, inner // QUARTERS, width), F32),
        ),
        in_specs=[VMEM, VMEM, SMEM],
        out_specs=[VMEM, VMEM],
        compiler_params=pltpu.CompilerParams(vmem_limit_bytes=12 << 20),
        name="query",
    )(tok, wq, level_weights)


def inside_kernel(width, first, q_ref, k_ref, v_ref, levels, after, inside_ref):
    rows, columns_here = inside_ref.shape
    block = rows // 2
    low = lax.broadcasted_iota(jnp.int32, (block, block), 0) >= lax.broadcasted_iota(
        jnp.int32, (block, block), 1
    )
    for local in range(columns_here // width):
        head = first + local
        columns = slice(head * width, (head + 1) * width)
        scale = levels[0, head]
        for i in range(2):
            here = slice(i * block, (i + 1) * block)
            q = q_ref[here, columns]

            def weigh(keys, masked):
                scores = lax.dot_general(
                    q, keys, (((1,), (1,)), ((), ())), preferred_element_type=F32
                )
                if masked:
                    scores = jnp.where(low, scores, 0.0)
                return (scores * scale).astype(BF16)

            out = dot(weigh(k_ref[here, columns], True), v_ref[here, columns])
            if i:
                out = out + dot(weigh(k_ref[:block, columns], False), v_ref[:block, columns])
            inside_ref[here, local * width : (local + 1) * width] = out


def inside_of(query, keys, values, level_weights, after, first, count, width):
    return pl.pallas_call(
        functools.partial(inside_kernel, width, first),
        out_shape=jax.ShapeDtypeStruct((query.shape[0], count * width), F32),
        in_specs=[VMEM, VMEM, VMEM, SMEM, ANY],
        out_specs=VMEM,
        compiler_params=pltpu.CompilerParams(vmem_limit_bytes=12 << 20),
        name="inside",
    )(query, keys, values, level_weights, after)


def gather_kernel(levels, *refs):
    near = refs[:4]
    crossed, mine, z1, z2, z3, local_ref = refs[4:]
    y, _, core, z = position()
    heads = levels.shape[1]
    part = mine.shape[0] // heads
    for head in range(heads):
        rows = slice(head * part, (head + 1) * part)

        def factor(level, present):
            return levels[level + 1, head] * (present * 2.0 ** (-0.5 * level))

        def read(ref):
            return ref[rows, :].astype(F32)

        far = (
            read(crossed)
            + factor(4, bit(core ^ 1, 0)) * read(mine)
            + factor(5, bit(z, 0)) * read(z1)
            + factor(6, bit(z, 1)) * (read(z2) + read(z3))
        )
        sides = [read(ref) for ref in near]
        for distance in range(4):
            target = y ^ distance
            local_ref[distance, rows, :] = (
                far
                + factor(0, bit(target, 0)) * sides[distance ^ 1]
                + factor(1, bit(target, 1)) * (sides[distance ^ 2] + sides[distance ^ 3])
            )


def gather_of(level_weights, near, others):
    shape = near[0].shape
    return pl.pallas_call(
        gather_kernel,
        out_shape=jax.ShapeDtypeStruct((4, *shape), F32),
        in_specs=[SMEM] + [VMEM] * 9,
        out_specs=VMEM,
        compiler_params=pltpu.CompilerParams(vmem_limit_bytes=4 << 20),
        name="gather",
    )(level_weights, *near, *others)


def mix_kernel(
    width, q_ref, low_ref, high_ref, own, one, two, three, wo, out_hbm, slices, attended, out, sems
):
    rows, inner = q_ref.shape
    part = width // QUARTERS
    pair = 2 * width
    y = lax.axis_index("grp") % QUARTERS
    for distance, source in enumerate((own, one, two, three)):
        slices[y ^ distance] = source[...]
    half = inner // 2
    zero = jnp.zeros((width, width), BF16)
    for j in range(inner // pair):
        halves = []
        insides = []
        for side in range(2):
            head = 2 * j + side
            state = jnp.concatenate(
                [slices[q, head * part : (head + 1) * part, :] for q in range(QUARTERS)], 0
            )
            halves.append(jnp.concatenate([zero, state] if side else [state, zero], 1))
            start = head * width
            insides.append(
                low_ref[:, start : start + width]
                if start < half
                else high_ref[:, start - half : start - half + width]
            )
        columns = slice(j * pair, (j + 1) * pair)
        earlier = dot(q_ref[:, columns], jnp.concatenate(halves, 0))
        attended[:, columns] = (jnp.concatenate(insides, 1) + earlier).astype(BF16)
    steps = sems.shape[0]
    block = out.shape[1] // steps
    copies = []
    for i in range(steps):
        columns = pl.ds(i * block, block)
        out[:, columns] = dot(attended[...], wo[:, columns]).astype(BF16)
        copy = pltpu.make_async_copy(out.at[:, columns], out_hbm.at[:, columns], sems.at[i])
        copy.start()
        copies.append(copy)
    for copy in copies:
        copy.wait()


def mixed_of(query, insides, pieces, w_output, width):
    rows, inner = query.shape
    wide = w_output.shape[1]
    return pl.pallas_call(
        functools.partial(mix_kernel, width),
        out_shape=jax.ShapeDtypeStruct((rows, wide), BF16),
        in_specs=[VMEM] * 8,
        out_specs=HBM,
        scratch_shapes=[
            pltpu.VMEM((QUARTERS, inner // QUARTERS, width), BF16),
            pltpu.VMEM((rows, inner), BF16),
            pltpu.VMEM((rows, wide), BF16),
            pltpu.SemaphoreType.DMA((6,)),
        ],
        compiler_params=pltpu.CompilerParams(vmem_limit_bytes=16 << 20),
        name="mix",
    )(query, *insides, *pieces, w_output)


AXES = ("seq", "grp")
CORE, Y, X, Z = 16, 1, 4, 32


def flip(value, mask):
    devices = lax.axis_size("seq") * lax.axis_size("grp")
    return lax.ppermute(value, AXES, [(source, source ^ mask) for source in range(devices)])


def plus(total, others):
    for other in others:
        total = total + other.astype(F32)
    return total


def per_device(tokens, w_query, w_key, w_value, w_output, level_weights):
    heads = level_weights.shape[1]
    width = w_query.shape[1] // heads
    half = heads // 2
    keys, values, tok, wq, *sent = states_of(tokens, w_key, w_value, w_query, heads, width)
    n2, n1, n3, n0 = (
        flip(sent[2], CORE | 2 * Y),
        flip(sent[1], CORE | Y),
        flip(sent[3], CORE | 3 * Y),
        flip(sent[0], CORE),
    )
    query, factors = query_of(tok, wq, level_weights, width)
    n2, n1, n3, n0, query, factors = lax.optimization_barrier((n2, n1, n3, n0, query, factors))
    near = (n0, n1, n2, n3)
    going = plus(n0.astype(F32), near[1:]).astype(BF16)

    x2, x1, x3 = (flip(going, CORE | distance * X) for distance in (2, 1, 3))
    own = flip(going, CORE)
    low = inside_of(query, keys, values, level_weights, going, 0, half, width)
    x2, x1, x3, own, low = lax.optimization_barrier((x2, x1, x3, own, low))
    total = plus(own.astype(F32), (x1, x2, x3))
    mine = total.astype(BF16)
    crossing = (factors[0] * x1.astype(F32) + factors[1] * plus(x2.astype(F32), (x3,))).astype(BF16)

    total = plus(total, (flip(mine, CORE),))
    going = total.astype(BF16)
    z3, z2, z1 = (flip(going, CORE | distance * Z) for distance in (3, 2, 1))
    crossed = flip(crossing, CORE)
    high = inside_of(query, keys, values, level_weights, going, half, half, width)
    z3, z2, z1, crossed, high = lax.optimization_barrier((z3, z2, z1, crossed, high))
    total = plus(total, (z1, z2, z3))

    past = flip(total.astype(BF16), CORE | 6 * Z)
    gathered = gather_of(level_weights, near, (crossed, mine, z1, z2, z3))
    past, gathered = lax.optimization_barrier((past, gathered))
    last = factors[2] * past.astype(F32)
    back = [(gathered[distance] + last).astype(BF16) for distance in range(4)]
    p2, p1, p3, p0 = lax.optimization_barrier(
        (
            flip(back[2], CORE | 2 * Y),
            flip(back[1], CORE | Y),
            flip(back[3], CORE | 3 * Y),
            flip(back[0], CORE),
        )
    )
    return mixed_of(query, (low, high), (p0, p1, p2, p3), w_output, width)


def solution(mesh):
    placed = (P(("seq", "grp"), None), P(), P(), P(), P(), P())
    return jax.shard_map(
        per_device, mesh=mesh, in_specs=placed, out_specs=P(("seq", "grp"), None), check_vma=False
    )
```

```python
import functools

import jax
import jax.numpy as jnp
from jax import lax
from jax.experimental import pallas as pl
from jax.experimental.pallas import tpu as pltpu
from jax.sharding import PartitionSpec as P

BF16 = jnp.bfloat16
F32 = jnp.float32
VMEM = pl.BlockSpec(memory_space=pltpu.VMEM)
SMEM = pl.BlockSpec(memory_space=pltpu.SMEM)
ANY = pl.BlockSpec(memory_space=pl.ANY)
HBM = pl.BlockSpec(memory_space=pltpu.HBM)
QUARTERS = 4


def unit(matrix):
    return (matrix * lax.rsqrt(jnp.sum(matrix * matrix, -1, keepdims=True) + 1e-06)).astype(BF16)


def unit_pair(matrix, width):
    return jnp.concatenate([unit(matrix[:, :width]), unit(matrix[:, width:])], 1)


def dot(a, b):
    return jnp.dot(a, b, preferred_element_type=F32)


def state_kernel(
    width,
    tok_hbm,
    wk_hbm,
    wv_hbm,
    wq_hbm,
    k_ref,
    v_ref,
    tok,
    wq,
    own,
    one,
    two,
    three,
    weights,
    slices,
    sums,
    sems,
):
    depth = tok.shape[1]
    pair = 2 * width
    part = width // QUARTERS
    chunks = 3
    chunk = depth // chunks
    count = 0

    def copy(source, target):
        nonlocal count
        count += 1
        return pltpu.make_async_copy(source, target, sems.at[count - 1])

    def columns(start, size):
        return pl.ds(start * pair, size * pair)

    first = []
    for i in range(chunks):
        rows = pl.ds(i * chunk, chunk)
        first.append(copy(tok_hbm.at[:, rows], tok.at[:, rows]))
        first.append(copy(wk_hbm.at[rows, columns(0, 2)], weights.at[0, rows]))
    second = [
        copy(wk_hbm.at[:, columns(2, 1)], weights.at[1, :, columns(0, 1)]),
        copy(wv_hbm.at[:, columns(0, 1)], weights.at[1, :, columns(1, 1)]),
    ]
    third = copy(wv_hbm.at[:, columns(1, 2)], weights.at[2])
    last = copy(wq_hbm, wq)
    for item in (*first, *second, third, last):
        item.start()

    def finish_keys(j, product):
        k_ref[:, j * pair : (j + 1) * pair] = unit_pair(product, width)

    def finish_values(j, product):
        here = slice(j * pair, (j + 1) * pair)
        values = product.astype(BF16)
        v_ref[:, here] = values
        both = lax.dot_general(
            k_ref[:, here], values, (((0,), (0,)), ((), ())), preferred_element_type=F32
        )
        for side in range(2):
            head = 2 * j + side
            state = both[side * width : (side + 1) * width, side * width : (side + 1) * width]
            for q in range(QUARTERS):
                slices[q, head * part : (head + 1) * part, :] = state[
                    q * part : (q + 1) * part
                ].astype(BF16)

    for i in range(chunks):
        first[2 * i].wait()
        first[2 * i + 1].wait()
        rows = slice(i * chunk, (i + 1) * chunk)
        product = dot(tok[:, rows], weights[0, rows])
        sums[0] = product if i == 0 else sums[0] + product
    for item in second:
        item.wait()
    sums[1] = dot(tok[...], weights[1])
    finish_keys(0, sums[0, :, :pair])
    finish_keys(1, sums[0, :, pair:])
    third.wait()
    sums[0] = dot(tok[...], weights[2])
    finish_keys(2, sums[1, :, :pair])
    finish_values(0, sums[1, :, pair:])
    finish_values(1, sums[0, :, :pair])
    finish_values(2, sums[0, :, pair:])
    y = lax.axis_index("grp") % QUARTERS
    for distance, target in enumerate((own, one, two, three)):
        target[...] = slices[y ^ distance]
    last.wait()


def states_of(tokens, w_key, w_value, w_query, heads, width):
    rows, depth = tokens.shape
    inner = heads * width
    piece = jax.ShapeDtypeStruct((inner // QUARTERS, width), BF16)
    side = jax.ShapeDtypeStruct((rows, inner), BF16)
    whole = [jax.ShapeDtypeStruct(a.shape, a.dtype) for a in (tokens, w_query)]
    operands = (tokens, w_key, w_value, w_query)
    return pl.pallas_call(
        functools.partial(state_kernel, width),
        out_shape=(side, side, *whole, piece, piece, piece, piece),
        in_specs=[HBM] * 4,
        out_specs=[VMEM] * 8,
        scratch_shapes=[
            pltpu.VMEM((3, depth, 4 * width), BF16),
            pltpu.VMEM((QUARTERS, inner // QUARTERS, width), BF16),
            pltpu.VMEM((2, rows, 4 * width), F32),
            pltpu.SemaphoreType.DMA((10,)),
        ],
        compiler_params=pltpu.CompilerParams(vmem_limit_bytes=24 << 20),
        name="states",
    )(*(pltpu.with_memory_space_constraint(operand, pltpu.HBM) for operand in operands))


def position():
    member = lax.axis_index("grp")
    group = lax.axis_index("seq")
    return member % 4, member // 4, group % 2, group // 2


def bit(index, level):
    return ((index >> level) & 1).astype(F32)


def query_kernel(width, tok, wq, q_ref):
    pair = 2 * width
    for j in range(wq.shape[1] // pair):
        columns = slice(j * pair, (j + 1) * pair)
        q_ref[:, columns] = unit_pair(dot(tok[...], wq[:, columns]), width)


def query_of(tok, wq, width):
    return pl.pallas_call(
        functools.partial(query_kernel, width),
        out_shape=jax.ShapeDtypeStruct((tok.shape[0], wq.shape[1]), BF16),
        in_specs=[VMEM, VMEM],
        out_specs=VMEM,
        compiler_params=pltpu.CompilerParams(vmem_limit_bytes=12 << 20),
        name="query",
    )(tok, wq)


def inside_kernel(width, first, q_ref, k_ref, v_ref, levels, after, inside_ref):
    rows, columns_here = inside_ref.shape
    block = rows // 2
    low = lax.broadcasted_iota(jnp.int32, (block, block), 0) >= lax.broadcasted_iota(
        jnp.int32, (block, block), 1
    )
    for local in range(columns_here // width):
        head = first + local
        columns = slice(head * width, (head + 1) * width)
        scale = levels[0, head]
        for i in range(2):
            here = slice(i * block, (i + 1) * block)
            q = q_ref[here, columns]

            def weigh(keys, masked):
                scores = lax.dot_general(
                    q, keys, (((1,), (1,)), ((), ())), preferred_element_type=F32
                )
                if masked:
                    scores = jnp.where(low, scores, 0.0)
                return (scores * scale).astype(BF16)

            out = dot(weigh(k_ref[here, columns], True), v_ref[here, columns])
            if i:
                out = out + dot(weigh(k_ref[:block, columns], False), v_ref[:block, columns])
            inside_ref[here, local * width : (local + 1) * width] = out


def inside_of(query, keys, values, level_weights, after, first, count, width):
    return pl.pallas_call(
        functools.partial(inside_kernel, width, first),
        out_shape=jax.ShapeDtypeStruct((query.shape[0], count * width), F32),
        in_specs=[VMEM, VMEM, VMEM, SMEM, ANY],
        out_specs=VMEM,
        compiler_params=pltpu.CompilerParams(vmem_limit_bytes=12 << 20),
        name="inside",
    )(query, keys, values, level_weights, after)


def gather_kernel(levels, *refs):
    near = refs[:4]
    crossed, mine, z1, z2, z3, local_ref, last_ref = refs[4:]
    y, x, core, z = position()
    heads = levels.shape[1]
    part = mine.shape[0] // heads
    for head in range(heads):
        rows = slice(head * part, (head + 1) * part)

        def factor(level, present):
            return levels[level + 1, head] * (present * 2.0 ** (-0.5 * level))

        def read(ref):
            return ref[rows, :].astype(F32)

        far = (
            factor(2, bit(x, 0)) * crossed[0, rows, :].astype(F32)
            + factor(3, bit(x, 1)) * crossed[1, rows, :].astype(F32)
            + factor(4, bit(core ^ 1, 0)) * read(mine)
            + factor(5, bit(z, 0)) * read(z1)
            + factor(6, bit(z, 1)) * (read(z2) + read(z3))
        )
        sides = [read(ref) for ref in near]
        for distance in range(4):
            target = y ^ distance
            local_ref[distance, rows, :] = (
                far
                + factor(0, bit(target, 0)) * sides[distance ^ 1]
                + factor(1, bit(target, 1)) * (sides[distance ^ 2] + sides[distance ^ 3])
            )
        last_ref[rows, :] = jnp.full((part, last_ref.shape[1]), factor(7, bit(z, 2)), F32)


def gather_of(level_weights, near, others):
    shape = near[0].shape
    return pl.pallas_call(
        gather_kernel,
        out_shape=(jax.ShapeDtypeStruct((4, *shape), F32), jax.ShapeDtypeStruct(shape, F32)),
        in_specs=[SMEM] + [VMEM] * 9,
        out_specs=[VMEM, VMEM],
        compiler_params=pltpu.CompilerParams(vmem_limit_bytes=4 << 20),
        name="gather",
    )(level_weights, *near, *others)


def mix_kernel(
    width, q_ref, low_ref, high_ref, own, one, two, three, wo, out_hbm, slices, attended, out, sems
):
    rows, inner = q_ref.shape
    part = width // QUARTERS
    pair = 2 * width
    y = lax.axis_index("grp") % QUARTERS
    for distance, source in enumerate((own, one, two, three)):
        slices[y ^ distance] = source[...]
    half = inner // 2
    zero = jnp.zeros((width, width), BF16)
    for j in range(inner // pair):
        halves = []
        insides = []
        for side in range(2):
            head = 2 * j + side
            state = jnp.concatenate(
                [slices[q, head * part : (head + 1) * part, :] for q in range(QUARTERS)], 0
            )
            halves.append(jnp.concatenate([zero, state] if side else [state, zero], 1))
            start = head * width
            insides.append(
                low_ref[:, start : start + width]
                if start < half
                else high_ref[:, start - half : start - half + width]
            )
        columns = slice(j * pair, (j + 1) * pair)
        earlier = dot(q_ref[:, columns], jnp.concatenate(halves, 0))
        attended[:, columns] = (jnp.concatenate(insides, 1) + earlier).astype(BF16)
    steps = sems.shape[0]
    block = out.shape[1] // steps
    copies = []
    for i in range(steps):
        columns = pl.ds(i * block, block)
        out[:, columns] = dot(attended[...], wo[:, columns]).astype(BF16)
        copy = pltpu.make_async_copy(out.at[:, columns], out_hbm.at[:, columns], sems.at[i])
        copy.start()
        copies.append(copy)
    for copy in copies:
        copy.wait()


def mixed_of(query, insides, pieces, w_output, width):
    rows, inner = query.shape
    wide = w_output.shape[1]
    return pl.pallas_call(
        functools.partial(mix_kernel, width),
        out_shape=jax.ShapeDtypeStruct((rows, wide), BF16),
        in_specs=[VMEM] * 8,
        out_specs=HBM,
        scratch_shapes=[
            pltpu.VMEM((QUARTERS, inner // QUARTERS, width), BF16),
            pltpu.VMEM((rows, inner), BF16),
            pltpu.VMEM((rows, wide), BF16),
            pltpu.SemaphoreType.DMA((6,)),
        ],
        compiler_params=pltpu.CompilerParams(vmem_limit_bytes=16 << 20),
        name="mix",
    )(query, *insides, *pieces, w_output)


AXES = ("seq", "grp")
CORE, Y, X, Z = 16, 1, 4, 32


def flip(value, mask):
    devices = lax.axis_size("seq") * lax.axis_size("grp")
    return lax.ppermute(value, AXES, [(source, source ^ mask) for source in range(devices)])


def plus(total, others):
    for other in others:
        total = total + other.astype(F32)
    return total


def per_device(tokens, w_query, w_key, w_value, w_output, level_weights):
    heads = level_weights.shape[1]
    width = w_query.shape[1] // heads
    half = heads // 2
    keys, values, tok, wq, *sent = states_of(tokens, w_key, w_value, w_query, heads, width)
    n2, n1, n3, n0 = (
        flip(sent[2], CORE | 2 * Y),
        flip(sent[1], CORE | Y),
        flip(sent[3], CORE | 3 * Y),
        flip(sent[0], CORE),
    )
    query = query_of(tok, wq, width)
    n2, n1, n3, n0, query = lax.optimization_barrier((n2, n1, n3, n0, query))
    near = (n0, n1, n2, n3)
    going = plus(n0.astype(F32), near[1:]).astype(BF16)

    x2, x1, x3 = (flip(going, CORE | distance * X) for distance in (2, 1, 3))
    own = flip(going, CORE)
    low = inside_of(query, keys, values, level_weights, going, 0, half, width)
    x2, x1, x3, own, low = lax.optimization_barrier((x2, x1, x3, own, low))
    total = plus(own.astype(F32), (x1, x2, x3))
    mine = total.astype(BF16)
    crossing = jnp.stack([x1.astype(F32), plus(x2.astype(F32), (x3,))]).astype(BF16)

    total = plus(total, (flip(mine, CORE),))
    going = total.astype(BF16)
    z1, z3, z2 = (flip(going, CORE | distance * Z) for distance in (1, 3, 2))
    high = inside_of(query, keys, values, level_weights, going, half, half, width)
    z1, z3, z2, high = lax.optimization_barrier((z1, z3, z2, high))
    going = plus(total, (z3, z2, z1)).astype(BF16)

    going, crossing = lax.optimization_barrier((going, crossing))
    crossed = flip(crossing, CORE)
    past = flip(going, CORE | 6 * Z)
    gathered, factor = gather_of(level_weights, near, (crossed, mine, z1, z2, z3))
    past, gathered, factor = lax.optimization_barrier((past, gathered, factor))
    last = factor * past.astype(F32)
    back = [(gathered[distance] + last).astype(BF16) for distance in range(4)]
    p2, p1, p3, p0 = lax.optimization_barrier(
        (
            flip(back[2], CORE | 2 * Y),
            flip(back[1], CORE | Y),
            flip(back[3], CORE | 3 * Y),
            flip(back[0], CORE),
        )
    )
    return mixed_of(query, (low, high), (p0, p1, p2, p3), w_output, width)


def solution(mesh):
    placed = (P(("seq", "grp"), None), P(), P(), P(), P(), P())
    return jax.shard_map(
        per_device, mesh=mesh, in_specs=placed, out_specs=P(("seq", "grp"), None), check_vma=False
    )
```

```python
import functools

import jax
import jax.numpy as jnp
from jax import lax
from jax.experimental import pallas as pl
from jax.experimental.pallas import tpu as pltpu
from jax.sharding import PartitionSpec as P

BF16 = jnp.bfloat16
F32 = jnp.float32
VMEM = pl.BlockSpec(memory_space=pltpu.VMEM)
SMEM = pl.BlockSpec(memory_space=pltpu.SMEM)
ANY = pl.BlockSpec(memory_space=pl.ANY)
HBM = pl.BlockSpec(memory_space=pltpu.HBM)
QUARTERS = 4


def unit(matrix):
    return (matrix * lax.rsqrt(jnp.sum(matrix * matrix, -1, keepdims=True) + 1e-06)).astype(BF16)


def unit_pair(matrix, width):
    return jnp.concatenate([unit(matrix[:, :width]), unit(matrix[:, width:])], 1)


def dot(a, b):
    return jnp.dot(a, b, preferred_element_type=F32)


def state_kernel(
    width,
    tok_hbm,
    wk_hbm,
    wv_hbm,
    wq_hbm,
    k_ref,
    v_ref,
    tok,
    wq,
    own,
    one,
    two,
    three,
    weights,
    slices,
    sums,
    sems,
):
    depth = tok.shape[1]
    pair = 2 * width
    part = width // QUARTERS
    chunks = 3
    chunk = depth // chunks
    count = 0

    def copy(source, target):
        nonlocal count
        count += 1
        return pltpu.make_async_copy(source, target, sems.at[count - 1])

    def columns(start, size):
        return pl.ds(start * pair, size * pair)

    first = []
    for i in range(chunks):
        rows = pl.ds(i * chunk, chunk)
        first.append(copy(tok_hbm.at[:, rows], tok.at[:, rows]))
        first.append(copy(wk_hbm.at[rows, columns(0, 2)], weights.at[0, rows]))
    second = [
        copy(wk_hbm.at[:, columns(2, 1)], weights.at[1, :, columns(0, 1)]),
        copy(wv_hbm.at[:, columns(0, 1)], weights.at[1, :, columns(1, 1)]),
    ]
    third = copy(wv_hbm.at[:, columns(1, 2)], weights.at[2])
    last = copy(wq_hbm, wq)
    for item in (*first, *second, third, last):
        item.start()

    def finish_keys(j, product):
        k_ref[:, j * pair : (j + 1) * pair] = unit_pair(product, width)

    def finish_values(j, product):
        here = slice(j * pair, (j + 1) * pair)
        values = product.astype(BF16)
        v_ref[:, here] = values
        both = lax.dot_general(
            k_ref[:, here], values, (((0,), (0,)), ((), ())), preferred_element_type=F32
        )
        for side in range(2):
            head = 2 * j + side
            state = both[side * width : (side + 1) * width, side * width : (side + 1) * width]
            for q in range(QUARTERS):
                slices[q, head * part : (head + 1) * part, :] = state[
                    q * part : (q + 1) * part
                ].astype(BF16)

    for i in range(chunks):
        first[2 * i].wait()
        first[2 * i + 1].wait()
        rows = slice(i * chunk, (i + 1) * chunk)
        product = dot(tok[:, rows], weights[0, rows])
        sums[0] = product if i == 0 else sums[0] + product
    for item in second:
        item.wait()
    sums[1] = dot(tok[...], weights[1])
    finish_keys(0, sums[0, :, :pair])
    finish_keys(1, sums[0, :, pair:])
    third.wait()
    sums[0] = dot(tok[...], weights[2])
    finish_keys(2, sums[1, :, :pair])
    finish_values(0, sums[1, :, pair:])
    finish_values(1, sums[0, :, :pair])
    finish_values(2, sums[0, :, pair:])
    y = lax.axis_index("grp") % QUARTERS
    for distance, target in enumerate((own, one, two, three)):
        target[...] = slices[y ^ distance]
    last.wait()


def states_of(tokens, w_key, w_value, w_query, heads, width):
    rows, depth = tokens.shape
    inner = heads * width
    piece = jax.ShapeDtypeStruct((inner // QUARTERS, width), BF16)
    side = jax.ShapeDtypeStruct((rows, inner), BF16)
    whole = [jax.ShapeDtypeStruct(a.shape, a.dtype) for a in (tokens, w_query)]
    operands = (tokens, w_key, w_value, w_query)
    return pl.pallas_call(
        functools.partial(state_kernel, width),
        out_shape=(side, side, *whole, piece, piece, piece, piece),
        in_specs=[HBM] * 4,
        out_specs=[VMEM] * 8,
        scratch_shapes=[
            pltpu.VMEM((3, depth, 4 * width), BF16),
            pltpu.VMEM((QUARTERS, inner // QUARTERS, width), BF16),
            pltpu.VMEM((2, rows, 4 * width), F32),
            pltpu.SemaphoreType.DMA((10,)),
        ],
        compiler_params=pltpu.CompilerParams(vmem_limit_bytes=24 << 20),
        name="states",
    )(*(pltpu.with_memory_space_constraint(operand, pltpu.HBM) for operand in operands))


def position():
    member = lax.axis_index("grp")
    group = lax.axis_index("seq")
    return member % 4, member // 4, group % 2, group // 2


def bit(index, level):
    return ((index >> level) & 1).astype(F32)


def query_kernel(width, tok, wq, q_ref):
    pair = 2 * width
    for j in range(wq.shape[1] // pair):
        columns = slice(j * pair, (j + 1) * pair)
        q_ref[:, columns] = unit_pair(dot(tok[...], wq[:, columns]), width)


def query_of(tok, wq, width):
    return pl.pallas_call(
        functools.partial(query_kernel, width),
        out_shape=jax.ShapeDtypeStruct((tok.shape[0], wq.shape[1]), BF16),
        in_specs=[VMEM, VMEM],
        out_specs=VMEM,
        compiler_params=pltpu.CompilerParams(vmem_limit_bytes=12 << 20),
        name="query",
    )(tok, wq)


def inside_kernel(width, first, q_ref, k_ref, v_ref, levels, after, inside_ref):
    rows, columns_here = inside_ref.shape
    block = rows // 2
    low = lax.broadcasted_iota(jnp.int32, (block, block), 0) >= lax.broadcasted_iota(
        jnp.int32, (block, block), 1
    )
    for local in range(columns_here // width):
        head = first + local
        columns = slice(head * width, (head + 1) * width)
        scale = levels[0, head]
        for i in range(2):
            here = slice(i * block, (i + 1) * block)
            q = q_ref[here, columns]

            def weigh(keys, masked):
                scores = lax.dot_general(
                    q, keys, (((1,), (1,)), ((), ())), preferred_element_type=F32
                )
                if masked:
                    scores = jnp.where(low, scores, 0.0)
                return (scores * scale).astype(BF16)

            out = dot(weigh(k_ref[here, columns], True), v_ref[here, columns])
            if i:
                out = out + dot(weigh(k_ref[:block, columns], False), v_ref[:block, columns])
            inside_ref[here, local * width : (local + 1) * width] = out


def inside_of(query, keys, values, level_weights, after, first, count, width):
    return pl.pallas_call(
        functools.partial(inside_kernel, width, first),
        out_shape=jax.ShapeDtypeStruct((query.shape[0], count * width), F32),
        in_specs=[VMEM, VMEM, VMEM, SMEM, ANY],
        out_specs=VMEM,
        compiler_params=pltpu.CompilerParams(vmem_limit_bytes=12 << 20),
        name="inside",
    )(query, keys, values, level_weights, after)


def gather_kernel(levels, *refs):
    near = refs[:4]
    crossed, mine, z1, z2, z3, local_ref, last_ref = refs[4:]
    y, x, core, z = position()
    heads = levels.shape[1]
    part = mine.shape[0] // heads
    for head in range(heads):
        rows = slice(head * part, (head + 1) * part)

        def factor(level, present):
            return levels[level + 1, head] * (present * 2.0 ** (-0.5 * level))

        def read(ref):
            return ref[rows, :].astype(F32)

        far = (
            factor(2, bit(x, 0)) * crossed[0, rows, :].astype(F32)
            + factor(3, bit(x, 1)) * crossed[1, rows, :].astype(F32)
            + factor(4, bit(core ^ 1, 0)) * read(mine)
            + factor(5, bit(z, 0)) * read(z1)
            + factor(6, bit(z, 1)) * (read(z2) + read(z3))
        )
        sides = [read(ref) for ref in near]
        for distance in range(4):
            target = y ^ distance
            local_ref[distance, rows, :] = (
                far
                + factor(0, bit(target, 0)) * sides[distance ^ 1]
                + factor(1, bit(target, 1)) * (sides[distance ^ 2] + sides[distance ^ 3])
            )
        last_ref[rows, :] = jnp.full((part, last_ref.shape[1]), factor(7, bit(z, 2)), F32)


def gather_of(level_weights, near, others):
    shape = near[0].shape
    return pl.pallas_call(
        gather_kernel,
        out_shape=(jax.ShapeDtypeStruct((4, *shape), F32), jax.ShapeDtypeStruct(shape, F32)),
        in_specs=[SMEM] + [VMEM] * 9,
        out_specs=[VMEM, VMEM],
        compiler_params=pltpu.CompilerParams(vmem_limit_bytes=4 << 20),
        name="gather",
    )(level_weights, *near, *others)


def mix_kernel(
    width, q_ref, low_ref, high_ref, own, one, two, three, wo, out_hbm, slices, attended, out, sems
):
    rows, inner = q_ref.shape
    part = width // QUARTERS
    pair = 2 * width
    y = lax.axis_index("grp") % QUARTERS
    for distance, source in enumerate((own, one, two, three)):
        slices[y ^ distance] = source[...]
    half = inner // 2
    zero = jnp.zeros((width, width), BF16)
    for j in range(inner // pair):
        halves = []
        insides = []
        for side in range(2):
            head = 2 * j + side
            state = jnp.concatenate(
                [slices[q, head * part : (head + 1) * part, :] for q in range(QUARTERS)], 0
            )
            halves.append(jnp.concatenate([zero, state] if side else [state, zero], 1))
            start = head * width
            insides.append(
                low_ref[:, start : start + width]
                if start < half
                else high_ref[:, start - half : start - half + width]
            )
        columns = slice(j * pair, (j + 1) * pair)
        earlier = dot(q_ref[:, columns], jnp.concatenate(halves, 0))
        attended[:, columns] = (jnp.concatenate(insides, 1) + earlier).astype(BF16)
    steps = sems.shape[0]
    block = out.shape[1] // steps
    copies = []
    for i in range(steps):
        columns = pl.ds(i * block, block)
        out[:, columns] = dot(attended[...], wo[:, columns]).astype(BF16)
        copy = pltpu.make_async_copy(out.at[:, columns], out_hbm.at[:, columns], sems.at[i])
        copy.start()
        copies.append(copy)
    for copy in copies:
        copy.wait()


def mixed_of(query, insides, pieces, w_output, width):
    rows, inner = query.shape
    wide = w_output.shape[1]
    return pl.pallas_call(
        functools.partial(mix_kernel, width),
        out_shape=jax.ShapeDtypeStruct((rows, wide), BF16),
        in_specs=[VMEM] * 8,
        out_specs=HBM,
        scratch_shapes=[
            pltpu.VMEM((QUARTERS, inner // QUARTERS, width), BF16),
            pltpu.VMEM((rows, inner), BF16),
            pltpu.VMEM((rows, wide), BF16),
            pltpu.SemaphoreType.DMA((6,)),
        ],
        compiler_params=pltpu.CompilerParams(vmem_limit_bytes=16 << 20),
        name="mix",
    )(query, *insides, *pieces, w_output)


AXES = ("seq", "grp")
CORE, Y, X, Z = 16, 1, 4, 32


def flip(value, mask):
    devices = lax.axis_size("seq") * lax.axis_size("grp")
    return lax.ppermute(value, AXES, [(source, source ^ mask) for source in range(devices)])


def plus(total, others):
    for other in others:
        total = total + other.astype(F32)
    return total


def per_device(tokens, w_query, w_key, w_value, w_output, level_weights):
    heads = level_weights.shape[1]
    width = w_query.shape[1] // heads
    half = heads // 2
    keys, values, tok, wq, *sent = states_of(tokens, w_key, w_value, w_query, heads, width)
    n2, n3, n1, n0 = (
        flip(sent[2], CORE | 2 * Y),
        flip(sent[3], CORE | 3 * Y),
        flip(sent[1], CORE | Y),
        flip(sent[0], CORE),
    )
    query = query_of(tok, wq, width)
    n2, n3, n1, n0, query = lax.optimization_barrier((n2, n3, n1, n0, query))
    near = (n0, n1, n2, n3)
    going = plus(n0.astype(F32), near[1:]).astype(BF16)

    x2, x3, x1 = (flip(going, CORE | distance * X) for distance in (2, 3, 1))
    own = flip(going, CORE)
    low = inside_of(query, keys, values, level_weights, going, 0, half, width)
    x2, x3, x1, own, low = lax.optimization_barrier((x2, x3, x1, own, low))
    total = plus(own.astype(F32), (x1, x2, x3))
    mine = total.astype(BF16)
    crossing = jnp.stack([x1.astype(F32), plus(x2.astype(F32), (x3,))]).astype(BF16)

    total = plus(total, (flip(mine, CORE),))
    going = total.astype(BF16)
    z1, z3, z2 = (flip(going, CORE | distance * Z) for distance in (1, 3, 2))
    high = inside_of(query, keys, values, level_weights, going, half, half, width)
    crossed = flip(crossing, CORE)
    crossed, z3, z2, z1, high = lax.optimization_barrier((crossed, z3, z2, z1, high))
    going = plus(total, (z3, z2, z1)).astype(BF16)

    going, crossing = lax.optimization_barrier((going, crossing))
    past = flip(going, CORE | 6 * Z)
    gathered, factor = gather_of(level_weights, near, (crossed, mine, z1, z2, z3))
    past, gathered, factor = lax.optimization_barrier((past, gathered, factor))
    last = factor * past.astype(F32)
    back = [(gathered[distance] + last).astype(BF16) for distance in range(4)]
    p2, p3, p1, p0 = lax.optimization_barrier(
        (
            flip(back[2], CORE | 2 * Y),
            flip(back[3], CORE | 3 * Y),
            flip(back[1], CORE | Y),
            flip(back[0], CORE),
        )
    )
    return mixed_of(query, (low, high), (p0, p1, p2, p3), w_output, width)


def solution(mesh):
    placed = (P(("seq", "grp"), None), P(), P(), P(), P(), P())
    return jax.shard_map(
        per_device, mesh=mesh, in_specs=placed, out_specs=P(("seq", "grp"), None), check_vma=False
    )
```

```python
import functools

import jax
import jax.numpy as jnp
from jax import lax
from jax.experimental import pallas as pl
from jax.experimental.pallas import tpu as pltpu
from jax.sharding import PartitionSpec as P

BF16 = jnp.bfloat16
F32 = jnp.float32
VMEM = pl.BlockSpec(memory_space=pltpu.VMEM)
SMEM = pl.BlockSpec(memory_space=pltpu.SMEM)
ANY = pl.BlockSpec(memory_space=pl.ANY)
HBM = pl.BlockSpec(memory_space=pltpu.HBM)
QUARTERS = 4


def unit(matrix):
    return (matrix * lax.rsqrt(jnp.sum(matrix * matrix, -1, keepdims=True) + 1e-06)).astype(BF16)


def unit_pair(matrix, width):
    return jnp.concatenate([unit(matrix[:, :width]), unit(matrix[:, width:])], 1)


def dot(a, b):
    return jnp.dot(a, b, preferred_element_type=F32)


def state_kernel(
    width,
    tok_hbm,
    wk_hbm,
    wv_hbm,
    wq_hbm,
    k_ref,
    v_ref,
    tok,
    wq,
    own,
    one,
    two,
    three,
    weights,
    slices,
    sums,
    sems,
):
    depth = tok.shape[1]
    pair = 2 * width
    part = width // QUARTERS
    chunks = 3
    chunk = depth // chunks
    count = 0

    def copy(source, target):
        nonlocal count
        count += 1
        return pltpu.make_async_copy(source, target, sems.at[count - 1])

    def columns(start, size):
        return pl.ds(start * pair, size * pair)

    first = []
    for i in range(chunks):
        rows = pl.ds(i * chunk, chunk)
        first.append(copy(tok_hbm.at[:, rows], tok.at[:, rows]))
        first.append(copy(wk_hbm.at[rows, columns(0, 2)], weights.at[0, rows]))
    second = [
        copy(wk_hbm.at[:, columns(2, 1)], weights.at[1, :, columns(0, 1)]),
        copy(wv_hbm.at[:, columns(0, 1)], weights.at[1, :, columns(1, 1)]),
    ]
    third = copy(wv_hbm.at[:, columns(1, 2)], weights.at[2])
    last = copy(wq_hbm, wq)
    for item in (*first, *second, third, last):
        item.start()

    def finish_keys(j, product):
        k_ref[:, j * pair : (j + 1) * pair] = unit_pair(product, width)

    def finish_values(j, product):
        here = slice(j * pair, (j + 1) * pair)
        values = product.astype(BF16)
        v_ref[:, here] = values
        both = lax.dot_general(
            k_ref[:, here], values, (((0,), (0,)), ((), ())), preferred_element_type=F32
        )
        for side in range(2):
            head = 2 * j + side
            state = both[side * width : (side + 1) * width, side * width : (side + 1) * width]
            for q in range(QUARTERS):
                slices[q, head * part : (head + 1) * part, :] = state[
                    q * part : (q + 1) * part
                ].astype(BF16)

    for i in range(chunks):
        first[2 * i].wait()
        first[2 * i + 1].wait()
        rows = slice(i * chunk, (i + 1) * chunk)
        product = dot(tok[:, rows], weights[0, rows])
        sums[0] = product if i == 0 else sums[0] + product
    for item in second:
        item.wait()
    sums[1] = dot(tok[...], weights[1])
    finish_keys(0, sums[0, :, :pair])
    finish_keys(1, sums[0, :, pair:])
    third.wait()
    sums[0] = dot(tok[...], weights[2])
    finish_keys(2, sums[1, :, :pair])
    finish_values(0, sums[1, :, pair:])
    finish_values(1, sums[0, :, :pair])
    finish_values(2, sums[0, :, pair:])
    y = lax.axis_index("grp") % QUARTERS
    for distance, target in enumerate((own, one, two, three)):
        target[...] = slices[y ^ distance]
    last.wait()


def states_of(tokens, w_key, w_value, w_query, heads, width):
    rows, depth = tokens.shape
    inner = heads * width
    piece = jax.ShapeDtypeStruct((inner // QUARTERS, width), BF16)
    side = jax.ShapeDtypeStruct((rows, inner), BF16)
    whole = [jax.ShapeDtypeStruct(a.shape, a.dtype) for a in (tokens, w_query)]
    operands = (tokens, w_key, w_value, w_query)
    return pl.pallas_call(
        functools.partial(state_kernel, width),
        out_shape=(side, side, *whole, piece, piece, piece, piece),
        in_specs=[HBM] * 4,
        out_specs=[VMEM] * 8,
        scratch_shapes=[
            pltpu.VMEM((3, depth, 4 * width), BF16),
            pltpu.VMEM((QUARTERS, inner // QUARTERS, width), BF16),
            pltpu.VMEM((2, rows, 4 * width), F32),
            pltpu.SemaphoreType.DMA((10,)),
        ],
        compiler_params=pltpu.CompilerParams(vmem_limit_bytes=24 << 20),
        name="states",
    )(*(pltpu.with_memory_space_constraint(operand, pltpu.HBM) for operand in operands))


def position():
    member = lax.axis_index("grp")
    group = lax.axis_index("seq")
    return member % 4, member // 4, group % 2, group // 2


def bit(index, level):
    return ((index >> level) & 1).astype(F32)


def query_kernel(width, tok, wq, q_ref):
    pair = 2 * width
    for j in range(wq.shape[1] // pair):
        columns = slice(j * pair, (j + 1) * pair)
        q_ref[:, columns] = unit_pair(dot(tok[...], wq[:, columns]), width)


def query_of(tok, wq, width):
    return pl.pallas_call(
        functools.partial(query_kernel, width),
        out_shape=jax.ShapeDtypeStruct((tok.shape[0], wq.shape[1]), BF16),
        in_specs=[VMEM, VMEM],
        out_specs=VMEM,
        compiler_params=pltpu.CompilerParams(vmem_limit_bytes=12 << 20),
        name="query",
    )(tok, wq)


def inside_kernel(width, first, q_ref, k_ref, v_ref, levels, after, inside_ref):
    rows, columns_here = inside_ref.shape
    block = rows // 2
    low = lax.broadcasted_iota(jnp.int32, (block, block), 0) >= lax.broadcasted_iota(
        jnp.int32, (block, block), 1
    )
    for local in range(columns_here // width):
        head = first + local
        columns = slice(head * width, (head + 1) * width)
        scale = levels[0, head]
        for i in range(2):
            here = slice(i * block, (i + 1) * block)
            q = q_ref[here, columns]

            def weigh(keys, masked):
                scores = lax.dot_general(
                    q, keys, (((1,), (1,)), ((), ())), preferred_element_type=F32
                )
                if masked:
                    scores = jnp.where(low, scores, 0.0)
                return (scores * scale).astype(BF16)

            out = dot(weigh(k_ref[here, columns], True), v_ref[here, columns])
            if i:
                out = out + dot(weigh(k_ref[:block, columns], False), v_ref[:block, columns])
            inside_ref[here, local * width : (local + 1) * width] = out


def inside_of(query, keys, values, level_weights, after, first, count, width):
    return pl.pallas_call(
        functools.partial(inside_kernel, width, first),
        out_shape=jax.ShapeDtypeStruct((query.shape[0], count * width), F32),
        in_specs=[VMEM, VMEM, VMEM, SMEM, ANY],
        out_specs=VMEM,
        compiler_params=pltpu.CompilerParams(vmem_limit_bytes=12 << 20),
        name="inside",
    )(query, keys, values, level_weights, after)


def gather_kernel(levels, *refs):
    near = refs[:4]
    crossed, mine, z1, z2, z3, local_ref, last_ref = refs[4:]
    y, x, core, z = position()
    heads = levels.shape[1]
    part = mine.shape[0] // heads
    for head in range(heads):
        rows = slice(head * part, (head + 1) * part)

        def factor(level, present):
            return levels[level + 1, head] * (present * 2.0 ** (-0.5 * level))

        def read(ref):
            return ref[rows, :].astype(F32)

        far = (
            factor(2, bit(x, 0)) * crossed[0, rows, :].astype(F32)
            + factor(3, bit(x, 1)) * crossed[1, rows, :].astype(F32)
            + factor(4, bit(core ^ 1, 0)) * read(mine)
            + factor(5, bit(z, 0)) * read(z1)
            + factor(6, bit(z, 1)) * (read(z2) + read(z3))
        )
        sides = [read(ref) for ref in near]
        for distance in range(4):
            target = y ^ distance
            local_ref[distance, rows, :] = (
                far
                + factor(0, bit(target, 0)) * sides[distance ^ 1]
                + factor(1, bit(target, 1)) * (sides[distance ^ 2] + sides[distance ^ 3])
            )
        last_ref[rows, :] = jnp.full((part, last_ref.shape[1]), factor(7, bit(z, 2)), F32)


def gather_of(level_weights, near, others):
    shape = near[0].shape
    return pl.pallas_call(
        gather_kernel,
        out_shape=(jax.ShapeDtypeStruct((4, *shape), F32), jax.ShapeDtypeStruct(shape, F32)),
        in_specs=[SMEM] + [VMEM] * 9,
        out_specs=[VMEM, VMEM],
        compiler_params=pltpu.CompilerParams(vmem_limit_bytes=4 << 20),
        name="gather",
    )(level_weights, *near, *others)


def mix_kernel(
    width, q_ref, low_ref, high_ref, own, one, two, three, wo, out_hbm, slices, attended, out, sems
):
    rows, inner = q_ref.shape
    part = width // QUARTERS
    pair = 2 * width
    y = lax.axis_index("grp") % QUARTERS
    for distance, source in enumerate((own, one, two, three)):
        slices[y ^ distance] = source[...]
    half = inner // 2
    zero = jnp.zeros((width, width), BF16)
    pairs = inner // pair

    def states(j):
        halves = []
        for side in range(2):
            head = 2 * j + side
            state = jnp.concatenate(
                [slices[q, head * part : (head + 1) * part, :] for q in range(QUARTERS)], 0
            )
            halves.append(jnp.concatenate([zero, state] if side else [state, zero], 1))
        return jnp.concatenate(halves, 0)

    def inside(here, start):
        ref, start = (low_ref, start) if start < half else (high_ref, start - half)
        return ref[here, start : start + width]

    blocks = 2
    height = rows // blocks
    steps = sems.shape[0] // blocks
    block = out.shape[1] // steps
    copies = []

    def attend(i):
        here = slice(i * height, (i + 1) * height)
        for j in range(pairs):
            columns = slice(j * pair, (j + 1) * pair)
            within = jnp.concatenate(
                [inside(here, j * pair), inside(here, j * pair + width)], 1
            )
            attended[here, columns] = (within + dot(q_ref[here, columns], states(j))).astype(BF16)

    def project(i):
        here = pl.ds(i * height, height)
        for step in range(steps):
            columns = pl.ds(step * block, block)
            out[here, columns] = dot(attended[here, :], wo[:, columns]).astype(BF16)
            copy = pltpu.make_async_copy(
                out.at[here, columns], out_hbm.at[here, columns], sems.at[len(copies)]
            )
            copy.start()
            copies.append(copy)

    attend(0)
    for i in range(blocks):
        if i + 1 < blocks:
            attend(i + 1)
        project(i)
    for copy in copies:
        copy.wait()


def mixed_of(query, insides, pieces, w_output, width):
    rows, inner = query.shape
    wide = w_output.shape[1]
    return pl.pallas_call(
        functools.partial(mix_kernel, width),
        out_shape=jax.ShapeDtypeStruct((rows, wide), BF16),
        in_specs=[VMEM] * 8,
        out_specs=HBM,
        scratch_shapes=[
            pltpu.VMEM((QUARTERS, inner // QUARTERS, width), BF16),
            pltpu.VMEM((rows, inner), BF16),
            pltpu.VMEM((rows, wide), BF16),
            pltpu.SemaphoreType.DMA((6,)),
        ],
        compiler_params=pltpu.CompilerParams(vmem_limit_bytes=16 << 20),
        name="mix",
    )(query, *insides, *pieces, w_output)


AXES = ("seq", "grp")
CORE, Y, X, Z = 16, 1, 4, 32


def flip(value, mask):
    devices = lax.axis_size("seq") * lax.axis_size("grp")
    return lax.ppermute(value, AXES, [(source, source ^ mask) for source in range(devices)])


def plus(total, others):
    for other in others:
        total = total + other.astype(F32)
    return total


def per_device(tokens, w_query, w_key, w_value, w_output, level_weights):
    heads = level_weights.shape[1]
    width = w_query.shape[1] // heads
    half = heads // 2
    keys, values, tok, wq, *sent = states_of(tokens, w_key, w_value, w_query, heads, width)
    n2, n3, n1, n0 = (
        flip(sent[2], CORE | 2 * Y),
        flip(sent[3], CORE | 3 * Y),
        flip(sent[1], CORE | Y),
        flip(sent[0], CORE),
    )
    query = query_of(tok, wq, width)
    n2, n3, n1, n0, query = lax.optimization_barrier((n2, n3, n1, n0, query))
    near = (n0, n1, n2, n3)
    going = plus(n0.astype(F32), near[1:]).astype(BF16)

    x2, x3, x1 = (flip(going, CORE | distance * X) for distance in (2, 3, 1))
    own = flip(going, CORE)
    low = inside_of(query, keys, values, level_weights, going, 0, half, width)
    x2, x3, x1, own, low = lax.optimization_barrier((x2, x3, x1, own, low))
    total = plus(own.astype(F32), (x1, x2, x3))
    mine = total.astype(BF16)
    crossing = jnp.stack([x1.astype(F32), plus(x2.astype(F32), (x3,))]).astype(BF16)

    total = plus(total, (flip(mine, CORE),))
    going = total.astype(BF16)
    z1, z3, z2 = (flip(going, CORE | distance * Z) for distance in (1, 3, 2))
    high = inside_of(query, keys, values, level_weights, going, half, half, width)
    crossing, high = lax.optimization_barrier((crossing, high))
    crossed = flip(crossing, CORE)
    z1, z3, z2, high = lax.optimization_barrier((z1, z3, z2, high))
    going = plus(total, (z3, z2, z1)).astype(BF16)

    going, crossing = lax.optimization_barrier((going, crossing))
    past = flip(going, CORE | 6 * Z)
    gathered, factor = gather_of(level_weights, near, (crossed, mine, z1, z2, z3))
    past, gathered, factor = lax.optimization_barrier((past, gathered, factor))
    last = factor * past.astype(F32)
    back = [(gathered[distance] + last).astype(BF16) for distance in range(4)]
    p2, p3, p1, p0 = lax.optimization_barrier(
        (
            flip(back[2], CORE | 2 * Y),
            flip(back[3], CORE | 3 * Y),
            flip(back[1], CORE | Y),
            flip(back[0], CORE),
        )
    )
    return mixed_of(query, (low, high), (p0, p1, p2, p3), w_output, width)


def solution(mesh):
    placed = (P(("seq", "grp"), None), P(), P(), P(), P(), P())
    return jax.shard_map(
        per_device, mesh=mesh, in_specs=placed, out_specs=P(("seq", "grp"), None), check_vma=False
    )
```

```python
import functools

import jax
import jax.numpy as jnp
from jax import lax
from jax.experimental import pallas as pl
from jax.experimental.pallas import tpu as pltpu
from jax.sharding import PartitionSpec as P

BF16 = jnp.bfloat16
F32 = jnp.float32
VMEM = pl.BlockSpec(memory_space=pltpu.VMEM)
SMEM = pl.BlockSpec(memory_space=pltpu.SMEM)
ANY = pl.BlockSpec(memory_space=pl.ANY)
HBM = pl.BlockSpec(memory_space=pltpu.HBM)
QUARTERS = 4


def unit(matrix):
    return (matrix * lax.rsqrt(jnp.sum(matrix * matrix, -1, keepdims=True) + 1e-06)).astype(BF16)


def unit_pair(matrix, width):
    return jnp.concatenate([unit(matrix[:, :width]), unit(matrix[:, width:])], 1)


def dot(a, b):
    return jnp.dot(a, b, preferred_element_type=F32)


def state_kernel(
    width,
    tok_hbm,
    wk_hbm,
    wv_hbm,
    wq_hbm,
    k_ref,
    v_ref,
    tok,
    wq,
    own,
    one,
    two,
    three,
    weights,
    slices,
    sums,
    sems,
):
    depth = tok.shape[1]
    pair = 2 * width
    part = width // QUARTERS
    chunks = 3
    chunk = depth // chunks
    count = 0

    def copy(source, target):
        nonlocal count
        count += 1
        return pltpu.make_async_copy(source, target, sems.at[count - 1])

    def columns(start, size):
        return pl.ds(start * pair, size * pair)

    first = []
    for i in range(chunks):
        rows = pl.ds(i * chunk, chunk)
        first.append(copy(tok_hbm.at[:, rows], tok.at[:, rows]))
        first.append(copy(wk_hbm.at[rows, columns(0, 2)], weights.at[0, rows]))
    second = [
        copy(wk_hbm.at[:, columns(2, 1)], weights.at[1, :, columns(0, 1)]),
        copy(wv_hbm.at[:, columns(0, 1)], weights.at[1, :, columns(1, 1)]),
    ]
    third = copy(wv_hbm.at[:, columns(1, 2)], weights.at[2])
    last = copy(wq_hbm, wq)
    for item in (*first, *second, third, last):
        item.start()

    def finish_keys(j, product):
        k_ref[:, j * pair : (j + 1) * pair] = unit_pair(product, width)

    def finish_values(j, product):
        here = slice(j * pair, (j + 1) * pair)
        values = product.astype(BF16)
        v_ref[:, here] = values
        both = lax.dot_general(
            k_ref[:, here], values, (((0,), (0,)), ((), ())), preferred_element_type=F32
        )
        for side in range(2):
            head = 2 * j + side
            state = both[side * width : (side + 1) * width, side * width : (side + 1) * width]
            for q in range(QUARTERS):
                slices[q, head * part : (head + 1) * part, :] = state[
                    q * part : (q + 1) * part
                ].astype(BF16)

    for i in range(chunks):
        first[2 * i].wait()
        first[2 * i + 1].wait()
        rows = slice(i * chunk, (i + 1) * chunk)
        product = dot(tok[:, rows], weights[0, rows])
        sums[0] = product if i == 0 else sums[0] + product
    for item in second:
        item.wait()
    sums[1] = dot(tok[...], weights[1])
    finish_keys(0, sums[0, :, :pair])
    finish_keys(1, sums[0, :, pair:])
    third.wait()
    sums[0] = dot(tok[...], weights[2])
    finish_keys(2, sums[1, :, :pair])
    finish_values(0, sums[1, :, pair:])
    finish_values(1, sums[0, :, :pair])
    finish_values(2, sums[0, :, pair:])
    y = lax.axis_index("grp") % QUARTERS
    for distance, target in enumerate((own, one, two, three)):
        target[...] = slices[y ^ distance]
    last.wait()


def states_of(tokens, w_key, w_value, w_query, heads, width):
    rows, depth = tokens.shape
    inner = heads * width
    piece = jax.ShapeDtypeStruct((inner // QUARTERS, width), BF16)
    side = jax.ShapeDtypeStruct((rows, inner), BF16)
    whole = [jax.ShapeDtypeStruct(a.shape, a.dtype) for a in (tokens, w_query)]
    operands = (tokens, w_key, w_value, w_query)
    return pl.pallas_call(
        functools.partial(state_kernel, width),
        out_shape=(side, side, *whole, piece, piece, piece, piece),
        in_specs=[HBM] * 4,
        out_specs=[VMEM] * 8,
        scratch_shapes=[
            pltpu.VMEM((3, depth, 4 * width), BF16),
            pltpu.VMEM((QUARTERS, inner // QUARTERS, width), BF16),
            pltpu.VMEM((2, rows, 4 * width), F32),
            pltpu.SemaphoreType.DMA((10,)),
        ],
        compiler_params=pltpu.CompilerParams(vmem_limit_bytes=24 << 20),
        name="states",
    )(*(pltpu.with_memory_space_constraint(operand, pltpu.HBM) for operand in operands))


def position():
    member = lax.axis_index("grp")
    group = lax.axis_index("seq")
    return member % 4, member // 4, group % 2, group // 2


def bit(index, level):
    return ((index >> level) & 1).astype(F32)


def query_kernel(width, tok, wq, q_ref):
    pair = 2 * width
    for j in range(wq.shape[1] // pair):
        columns = slice(j * pair, (j + 1) * pair)
        q_ref[:, columns] = unit_pair(dot(tok[...], wq[:, columns]), width)


def query_of(tok, wq, width):
    return pl.pallas_call(
        functools.partial(query_kernel, width),
        out_shape=jax.ShapeDtypeStruct((tok.shape[0], wq.shape[1]), BF16),
        in_specs=[VMEM, VMEM],
        out_specs=VMEM,
        compiler_params=pltpu.CompilerParams(vmem_limit_bytes=12 << 20),
        name="query",
    )(tok, wq)


def inside_kernel(width, first, q_ref, k_ref, v_ref, levels, after, inside_ref):
    rows, columns_here = inside_ref.shape
    block = rows // 2
    low = lax.broadcasted_iota(jnp.int32, (block, block), 0) >= lax.broadcasted_iota(
        jnp.int32, (block, block), 1
    )
    for local in range(columns_here // width):
        head = first + local
        columns = slice(head * width, (head + 1) * width)
        scale = levels[0, head]
        for i in range(2):
            here = slice(i * block, (i + 1) * block)
            q = q_ref[here, columns]

            def weigh(keys, masked):
                scores = lax.dot_general(
                    q, keys, (((1,), (1,)), ((), ())), preferred_element_type=F32
                )
                if masked:
                    scores = jnp.where(low, scores, 0.0)
                return (scores * scale).astype(BF16)

            out = dot(weigh(k_ref[here, columns], True), v_ref[here, columns])
            if i:
                out = out + dot(weigh(k_ref[:block, columns], False), v_ref[:block, columns])
            inside_ref[here, local * width : (local + 1) * width] = out


def inside_of(query, keys, values, level_weights, after, first, count, width):
    return pl.pallas_call(
        functools.partial(inside_kernel, width, first),
        out_shape=jax.ShapeDtypeStruct((query.shape[0], count * width), F32),
        in_specs=[VMEM, VMEM, VMEM, SMEM, ANY],
        out_specs=VMEM,
        compiler_params=pltpu.CompilerParams(vmem_limit_bytes=12 << 20),
        name="inside",
    )(query, keys, values, level_weights, after)


def gather_kernel(levels, *refs):
    near = refs[:4]
    x1, x2, x3, mine, z1, z2, z3, local_ref, last_ref = refs[4:]
    y, x, core, z = position()
    heads = levels.shape[1]
    part = mine.shape[0] // heads
    for head in range(heads):
        rows = slice(head * part, (head + 1) * part)

        def factor(level, present):
            return levels[level + 1, head] * (present * 2.0 ** (-0.5 * level))

        def read(ref):
            return ref[rows, :].astype(F32)

        far = (
            factor(2, bit(x, 0)) * x1[1, rows, :].astype(F32)
            + factor(3, bit(x, 1)) * (read(x2) + x3[1, rows, :].astype(F32))
            + factor(4, bit(core ^ 1, 0)) * read(mine)
            + factor(5, bit(z, 0)) * read(z1)
            + factor(6, bit(z, 1)) * (read(z2) + read(z3))
        )
        sides = [read(ref) for ref in near]
        for distance in range(4):
            target = y ^ distance
            local_ref[distance, rows, :] = (
                far
                + factor(0, bit(target, 0)) * sides[distance ^ 1]
                + factor(1, bit(target, 1)) * (sides[distance ^ 2] + sides[distance ^ 3])
            )
        last_ref[rows, :] = jnp.full((part, last_ref.shape[1]), factor(7, bit(z, 2)), F32)


def gather_of(level_weights, near, others):
    shape = near[0].shape
    return pl.pallas_call(
        gather_kernel,
        out_shape=(jax.ShapeDtypeStruct((4, *shape), F32), jax.ShapeDtypeStruct(shape, F32)),
        in_specs=[SMEM] + [VMEM] * 11,
        out_specs=[VMEM, VMEM],
        compiler_params=pltpu.CompilerParams(vmem_limit_bytes=4 << 20),
        name="gather",
    )(level_weights, *near, *others)


def mix_kernel(
    width, q_ref, low_ref, high_ref, own, one, two, three, wo, out_hbm, slices, attended, out, sems
):
    rows, inner = q_ref.shape
    part = width // QUARTERS
    pair = 2 * width
    y = lax.axis_index("grp") % QUARTERS
    for distance, source in enumerate((own, one, two, three)):
        slices[y ^ distance] = source[...]
    half = inner // 2
    zero = jnp.zeros((width, width), BF16)
    pairs = inner // pair

    def states(j):
        halves = []
        for side in range(2):
            head = 2 * j + side
            state = jnp.concatenate(
                [slices[q, head * part : (head + 1) * part, :] for q in range(QUARTERS)], 0
            )
            halves.append(jnp.concatenate([zero, state] if side else [state, zero], 1))
        return jnp.concatenate(halves, 0)

    def inside(here, start):
        ref, start = (low_ref, start) if start < half else (high_ref, start - half)
        return ref[here, start : start + width]

    blocks = 2
    height = rows // blocks
    steps = sems.shape[0] // blocks
    block = out.shape[1] // steps
    copies = []

    def attend(i):
        here = slice(i * height, (i + 1) * height)
        for j in range(pairs):
            columns = slice(j * pair, (j + 1) * pair)
            within = jnp.concatenate(
                [inside(here, j * pair), inside(here, j * pair + width)], 1
            )
            attended[here, columns] = (within + dot(q_ref[here, columns], states(j))).astype(BF16)

    def project(i):
        here = pl.ds(i * height, height)
        for step in range(steps):
            columns = pl.ds(step * block, block)
            out[here, columns] = dot(attended[here, :], wo[:, columns]).astype(BF16)
            copy = pltpu.make_async_copy(
                out.at[here, columns], out_hbm.at[here, columns], sems.at[len(copies)]
            )
            copy.start()
            copies.append(copy)

    attend(0)
    for i in range(blocks):
        if i + 1 < blocks:
            attend(i + 1)
        project(i)
    for copy in copies:
        copy.wait()


def mixed_of(query, insides, pieces, w_output, width):
    rows, inner = query.shape
    wide = w_output.shape[1]
    return pl.pallas_call(
        functools.partial(mix_kernel, width),
        out_shape=jax.ShapeDtypeStruct((rows, wide), BF16),
        in_specs=[VMEM] * 8,
        out_specs=HBM,
        scratch_shapes=[
            pltpu.VMEM((QUARTERS, inner // QUARTERS, width), BF16),
            pltpu.VMEM((rows, inner), BF16),
            pltpu.VMEM((rows, wide), BF16),
            pltpu.SemaphoreType.DMA((6,)),
        ],
        compiler_params=pltpu.CompilerParams(vmem_limit_bytes=16 << 20),
        name="mix",
    )(query, *insides, *pieces, w_output)


AXES = ("seq", "grp")
CORE, Y, X, Z = 16, 1, 4, 32


def flip(value, mask):
    devices = lax.axis_size("seq") * lax.axis_size("grp")
    return lax.ppermute(value, AXES, [(source, source ^ mask) for source in range(devices)])


def plus(total, others):
    for other in others:
        total = total + other.astype(F32)
    return total


def per_device(tokens, w_query, w_key, w_value, w_output, level_weights):
    heads = level_weights.shape[1]
    width = w_query.shape[1] // heads
    half = heads // 2
    keys, values, tok, wq, *sent = states_of(tokens, w_key, w_value, w_query, heads, width)
    n2, n3, n1, n0 = (
        flip(sent[2], CORE | 2 * Y),
        flip(sent[3], CORE | 3 * Y),
        flip(sent[1], CORE | Y),
        flip(sent[0], CORE),
    )
    query = query_of(tok, wq, width)
    n2, n3, n1, n0, query = lax.optimization_barrier((n2, n3, n1, n0, query))
    near = (n0, n1, n2, n3)
    total = plus(n0.astype(F32), near[1:])
    going = total.astype(BF16)

    own = flip(going, CORE)
    x2 = flip(going, CORE | 2 * X)
    both = jnp.stack([going, own])
    x3, x1 = flip(both, CORE | 3 * X), flip(both, CORE | X)
    other2 = flip(x2, CORE)
    low = inside_of(query, keys, values, level_weights, x2, 0, half, width)
    other2, x3, x1, low = lax.optimization_barrier((other2, x3, x1, low))
    mine = plus(own.astype(F32), (x1[0], x2, x3[0]))
    total = plus(total + mine, (x1[1], other2, x3[1]))
    mine = mine.astype(BF16)
    going = total.astype(BF16)
    z1, z3, z2 = (flip(going, CORE | distance * Z) for distance in (1, 3, 2))
    high = inside_of(query, keys, values, level_weights, going, half, half, width)
    z1, z3, z2, high = lax.optimization_barrier((z1, z3, z2, high))
    going = plus(total, (z3, z2, z1)).astype(BF16)

    past = flip(going, CORE | 6 * Z)
    gathered, factor = gather_of(level_weights, near, (x1, other2, x3, mine, z1, z2, z3))
    past, gathered, factor = lax.optimization_barrier((past, gathered, factor))
    last = factor * past.astype(F32)
    back = [(gathered[distance] + last).astype(BF16) for distance in range(4)]
    p2, p3, p1, p0 = lax.optimization_barrier(
        (
            flip(back[2], CORE | 2 * Y),
            flip(back[3], CORE | 3 * Y),
            flip(back[1], CORE | Y),
            flip(back[0], CORE),
        )
    )
    return mixed_of(query, (low, high), (p0, p1, p2, p3), w_output, width)


def solution(mesh):
    placed = (P(("seq", "grp"), None), P(), P(), P(), P(), P())
    return jax.shard_map(
        per_device, mesh=mesh, in_specs=placed, out_specs=P(("seq", "grp"), None), check_vma=False
    )
```

```python
import functools

import jax
import jax.numpy as jnp
from jax import lax
from jax.experimental import pallas as pl
from jax.experimental.pallas import tpu as pltpu
from jax.sharding import PartitionSpec as P

BF16 = jnp.bfloat16
F32 = jnp.float32
VMEM = pl.BlockSpec(memory_space=pltpu.VMEM)
SMEM = pl.BlockSpec(memory_space=pltpu.SMEM)
ANY = pl.BlockSpec(memory_space=pl.ANY)
HBM = pl.BlockSpec(memory_space=pltpu.HBM)
QUARTERS = 4


def unit(matrix):
    return (matrix * lax.rsqrt(jnp.sum(matrix * matrix, -1, keepdims=True) + 1e-06)).astype(BF16)


def unit_pair(matrix, width):
    return jnp.concatenate([unit(matrix[:, :width]), unit(matrix[:, width:])], 1)


def dot(a, b):
    return jnp.dot(a, b, preferred_element_type=F32)


def state_kernel(
    width,
    tok_hbm,
    wk_hbm,
    wv_hbm,
    wq_hbm,
    k_ref,
    v_ref,
    tok,
    wq,
    own,
    one,
    two,
    three,
    weights,
    slices,
    sums,
    sems,
):
    depth = tok.shape[1]
    pair = 2 * width
    part = width // QUARTERS
    chunks = 3
    chunk = depth // chunks
    count = 0

    def copy(source, target):
        nonlocal count
        count += 1
        return pltpu.make_async_copy(source, target, sems.at[count - 1])

    def columns(start, size):
        return pl.ds(start * pair, size * pair)

    first = []
    for i in range(chunks):
        rows = pl.ds(i * chunk, chunk)
        first.append(copy(tok_hbm.at[:, rows], tok.at[:, rows]))
        first.append(copy(wk_hbm.at[rows, columns(0, 2)], weights.at[0, rows]))
    second = [
        copy(wk_hbm.at[:, columns(2, 1)], weights.at[1, :, columns(0, 1)]),
        copy(wv_hbm.at[:, columns(0, 1)], weights.at[1, :, columns(1, 1)]),
    ]
    third = copy(wv_hbm.at[:, columns(1, 2)], weights.at[2])
    last = copy(wq_hbm, wq)
    for item in (*first, *second, third, last):
        item.start()

    def finish_keys(j, product):
        k_ref[:, j * pair : (j + 1) * pair] = unit_pair(product, width)

    def finish_values(j, product):
        here = slice(j * pair, (j + 1) * pair)
        values = product.astype(BF16)
        v_ref[:, here] = values
        both = lax.dot_general(
            k_ref[:, here], values, (((0,), (0,)), ((), ())), preferred_element_type=F32
        )
        for side in range(2):
            head = 2 * j + side
            state = both[side * width : (side + 1) * width, side * width : (side + 1) * width]
            for q in range(QUARTERS):
                slices[q, head * part : (head + 1) * part, :] = state[
                    q * part : (q + 1) * part
                ].astype(BF16)

    for i in range(chunks):
        first[2 * i].wait()
        first[2 * i + 1].wait()
        rows = slice(i * chunk, (i + 1) * chunk)
        product = dot(tok[:, rows], weights[0, rows])
        sums[0] = product if i == 0 else sums[0] + product
    for item in second:
        item.wait()
    sums[1] = dot(tok[...], weights[1])
    finish_keys(0, sums[0, :, :pair])
    finish_keys(1, sums[0, :, pair:])
    third.wait()
    sums[0] = dot(tok[...], weights[2])
    finish_keys(2, sums[1, :, :pair])
    finish_values(0, sums[1, :, pair:])
    finish_values(1, sums[0, :, :pair])
    finish_values(2, sums[0, :, pair:])
    y = lax.axis_index("grp") % QUARTERS
    for distance, target in enumerate((own, one, two, three)):
        target[...] = slices[y ^ distance]
    last.wait()


def states_of(tokens, w_key, w_value, w_query, heads, width):
    rows, depth = tokens.shape
    inner = heads * width
    piece = jax.ShapeDtypeStruct((inner // QUARTERS, width), BF16)
    side = jax.ShapeDtypeStruct((rows, inner), BF16)
    whole = [jax.ShapeDtypeStruct(a.shape, a.dtype) for a in (tokens, w_query)]
    operands = (tokens, w_key, w_value, w_query)
    return pl.pallas_call(
        functools.partial(state_kernel, width),
        out_shape=(side, side, *whole, piece, piece, piece, piece),
        in_specs=[HBM] * 4,
        out_specs=[VMEM] * 8,
        scratch_shapes=[
            pltpu.VMEM((3, depth, 4 * width), BF16),
            pltpu.VMEM((QUARTERS, inner // QUARTERS, width), BF16),
            pltpu.VMEM((2, rows, 4 * width), F32),
            pltpu.SemaphoreType.DMA((10,)),
        ],
        compiler_params=pltpu.CompilerParams(vmem_limit_bytes=24 << 20),
        name="states",
    )(*(pltpu.with_memory_space_constraint(operand, pltpu.HBM) for operand in operands))


def position():
    member = lax.axis_index("grp")
    group = lax.axis_index("seq")
    return member % 4, member // 4, group % 2, group // 2


def bit(index, level):
    return ((index >> level) & 1).astype(F32)


def query_kernel(width, tok, wq, q_ref):
    pair = 2 * width
    for j in range(wq.shape[1] // pair):
        columns = slice(j * pair, (j + 1) * pair)
        q_ref[:, columns] = unit_pair(dot(tok[...], wq[:, columns]), width)


def query_of(tok, wq, width):
    return pl.pallas_call(
        functools.partial(query_kernel, width),
        out_shape=jax.ShapeDtypeStruct((tok.shape[0], wq.shape[1]), BF16),
        in_specs=[VMEM, VMEM],
        out_specs=VMEM,
        compiler_params=pltpu.CompilerParams(vmem_limit_bytes=12 << 20),
        name="query",
    )(tok, wq)


def inside_kernel(width, first, q_ref, k_ref, v_ref, levels, after, inside_ref):
    rows, columns_here = inside_ref.shape
    block = rows // 2
    low = lax.broadcasted_iota(jnp.int32, (block, block), 0) >= lax.broadcasted_iota(
        jnp.int32, (block, block), 1
    )
    for local in range(columns_here // width):
        head = first + local
        columns = slice(head * width, (head + 1) * width)
        scale = levels[0, head]
        for i in range(2):
            here = slice(i * block, (i + 1) * block)
            q = q_ref[here, columns]

            def weigh(keys, masked):
                scores = lax.dot_general(
                    q, keys, (((1,), (1,)), ((), ())), preferred_element_type=F32
                )
                if masked:
                    scores = jnp.where(low, scores, 0.0)
                return (scores * scale).astype(BF16)

            out = dot(weigh(k_ref[here, columns], True), v_ref[here, columns])
            if i:
                out = out + dot(weigh(k_ref[:block, columns], False), v_ref[:block, columns])
            inside_ref[here, local * width : (local + 1) * width] = out


def inside_of(query, keys, values, level_weights, after, first, count, width):
    return pl.pallas_call(
        functools.partial(inside_kernel, width, first),
        out_shape=jax.ShapeDtypeStruct((query.shape[0], count * width), F32),
        in_specs=[VMEM, VMEM, VMEM, SMEM, ANY],
        out_specs=VMEM,
        compiler_params=pltpu.CompilerParams(vmem_limit_bytes=12 << 20),
        name="inside",
    )(query, keys, values, level_weights, after)


def gather_kernel(levels, *refs):
    near = refs[:4]
    x1, x2, x3, mine, z1, z2, z3, local_ref, last_ref = refs[4:]
    y, x, core, z = position()
    heads = levels.shape[1]
    part = mine.shape[0] // heads
    for head in range(heads):
        rows = slice(head * part, (head + 1) * part)

        def factor(level, present):
            return levels[level + 1, head] * (present * 2.0 ** (-0.5 * level))

        def read(ref):
            return ref[rows, :].astype(F32)

        far = (
            factor(2, bit(x, 0)) * x1[1, rows, :].astype(F32)
            + factor(3, bit(x, 1)) * (read(x2) + x3[1, rows, :].astype(F32))
            + factor(4, bit(core ^ 1, 0)) * read(mine)
            + factor(5, bit(z, 0)) * read(z1)
            + factor(6, bit(z, 1)) * (read(z2) + read(z3))
        )
        sides = [read(ref) for ref in near]
        for distance in range(4):
            target = y ^ distance
            local_ref[distance, rows, :] = (
                far
                + factor(0, bit(target, 0)) * sides[distance ^ 1]
                + factor(1, bit(target, 1)) * (sides[distance ^ 2] + sides[distance ^ 3])
            )
        last_ref[rows, :] = jnp.full((part, last_ref.shape[1]), factor(7, bit(z, 2)), F32)


def gather_of(level_weights, near, others):
    shape = near[0].shape
    return pl.pallas_call(
        gather_kernel,
        out_shape=(jax.ShapeDtypeStruct((4, *shape), F32), jax.ShapeDtypeStruct(shape, F32)),
        in_specs=[SMEM] + [VMEM] * 11,
        out_specs=[VMEM, VMEM],
        compiler_params=pltpu.CompilerParams(vmem_limit_bytes=4 << 20),
        name="gather",
    )(level_weights, *near, *others)


def mix_kernel(
    width, q_ref, low_ref, high_ref, own, one, two, three, wo, out_hbm, slices, attended, out, sems
):
    rows, inner = q_ref.shape
    part = width // QUARTERS
    pair = 2 * width
    y = lax.axis_index("grp") % QUARTERS
    for distance, source in enumerate((own, one, two, three)):
        slices[y ^ distance] = source[...]
    half = inner // 2
    zero = jnp.zeros((width, width), BF16)
    pairs = inner // pair

    def states(j):
        halves = []
        for side in range(2):
            head = 2 * j + side
            state = jnp.concatenate(
                [slices[q, head * part : (head + 1) * part, :] for q in range(QUARTERS)], 0
            )
            halves.append(jnp.concatenate([zero, state] if side else [state, zero], 1))
        return jnp.concatenate(halves, 0)

    def inside(here, start):
        ref, start = (low_ref, start) if start < half else (high_ref, start - half)
        return ref[here, start : start + width]

    blocks = 2
    height = rows // blocks
    steps = sems.shape[0] // blocks
    block = out.shape[1] // steps
    copies = []

    def attend(i):
        here = slice(i * height, (i + 1) * height)
        for j in range(pairs):
            columns = slice(j * pair, (j + 1) * pair)
            within = jnp.concatenate(
                [inside(here, j * pair), inside(here, j * pair + width)], 1
            )
            attended[here, columns] = (within + dot(q_ref[here, columns], states(j))).astype(BF16)

    def project(i):
        here = pl.ds(i * height, height)
        for step in range(steps):
            columns = pl.ds(step * block, block)
            out[here, columns] = dot(attended[here, :], wo[:, columns]).astype(BF16)
            copy = pltpu.make_async_copy(
                out.at[here, columns], out_hbm.at[here, columns], sems.at[len(copies)]
            )
            copy.start()
            copies.append(copy)

    attend(0)
    for i in range(blocks):
        if i + 1 < blocks:
            attend(i + 1)
        project(i)
    for copy in copies:
        copy.wait()


def mixed_of(query, insides, pieces, w_output, width):
    rows, inner = query.shape
    wide = w_output.shape[1]
    return pl.pallas_call(
        functools.partial(mix_kernel, width),
        out_shape=jax.ShapeDtypeStruct((rows, wide), BF16),
        in_specs=[VMEM] * 8,
        out_specs=HBM,
        scratch_shapes=[
            pltpu.VMEM((QUARTERS, inner // QUARTERS, width), BF16),
            pltpu.VMEM((rows, inner), BF16),
            pltpu.VMEM((rows, wide), BF16),
            pltpu.SemaphoreType.DMA((6,)),
        ],
        compiler_params=pltpu.CompilerParams(vmem_limit_bytes=16 << 20),
        name="mix",
    )(query, *insides, *pieces, w_output)


AXES = ("seq", "grp")
CORE, Y, X, Z = 16, 1, 4, 32


def flip(value, mask):
    devices = lax.axis_size("seq") * lax.axis_size("grp")
    return lax.ppermute(value, AXES, [(source, source ^ mask) for source in range(devices)])


def plus(total, others):
    for other in others:
        total = total + other.astype(F32)
    return total


def per_device(tokens, w_query, w_key, w_value, w_output, level_weights):
    heads = level_weights.shape[1]
    width = w_query.shape[1] // heads
    half = heads // 2
    keys, values, tok, wq, *sent = states_of(tokens, w_key, w_value, w_query, heads, width)
    n2, n3, n1, n0 = (
        flip(sent[2], CORE | 2 * Y),
        flip(sent[3], CORE | 3 * Y),
        flip(sent[1], CORE | Y),
        flip(sent[0], CORE),
    )
    query = query_of(tok, wq, width)
    n2, n3, n1, n0, query = lax.optimization_barrier((n2, n3, n1, n0, query))
    near = (n0, n1, n2, n3)
    total = plus(n0.astype(F32), near[1:])
    going = total.astype(BF16)

    own = flip(going, CORE)
    x2 = flip(going, CORE | 2 * X)
    both = jnp.stack([going, own])
    x3, x1 = flip(both, CORE | 3 * X), flip(both, CORE | X)
    other2 = flip(x2, CORE)
    other2, x3, x1 = lax.optimization_barrier((other2, x3, x1))
    mine = plus(own.astype(F32), (x1[0], x2, x3[0]))
    total = plus(total + mine, (x1[1], other2, x3[1]))
    mine = mine.astype(BF16)
    going = total.astype(BF16)
    z1, z3, z2 = (flip(going, CORE | distance * Z) for distance in (1, 3, 2))
    high = inside_of(query, keys, values, level_weights, going, half, half, width)
    z1, z3, z2, high = lax.optimization_barrier((z1, z3, z2, high))
    going = plus(total, (z3, z2, z1)).astype(BF16)

    past = flip(going, CORE | 6 * Z)
    gathered, factor = gather_of(level_weights, near, (x1, other2, x3, mine, z1, z2, z3))
    past, gathered, factor = lax.optimization_barrier((past, gathered, factor))
    last = factor * past.astype(F32)
    back = [(gathered[distance] + last).astype(BF16) for distance in range(4)]
    p2, p3, p1, p0 = (
        flip(back[2], CORE | 2 * Y),
        flip(back[3], CORE | 3 * Y),
        flip(back[1], CORE | Y),
        flip(back[0], CORE),
    )
    low = inside_of(query, keys, values, level_weights, back[0], 0, half, width)
    p2, p3, p1, p0, low = lax.optimization_barrier((p2, p3, p1, p0, low))
    return mixed_of(query, (low, high), (p0, p1, p2, p3), w_output, width)


def solution(mesh):
    placed = (P(("seq", "grp"), None), P(), P(), P(), P(), P())
    return jax.shard_map(
        per_device, mesh=mesh, in_specs=placed, out_specs=P(("seq", "grp"), None), check_vma=False
    )
```

```python
import functools

import jax
import jax.numpy as jnp
from jax import lax
from jax.experimental import pallas as pl
from jax.experimental.pallas import tpu as pltpu
from jax.sharding import PartitionSpec as P

BF16 = jnp.bfloat16
F32 = jnp.float32
VMEM = pl.BlockSpec(memory_space=pltpu.VMEM)
SMEM = pl.BlockSpec(memory_space=pltpu.SMEM)
ANY = pl.BlockSpec(memory_space=pl.ANY)
HBM = pl.BlockSpec(memory_space=pltpu.HBM)
QUARTERS = 4


def unit(matrix):
    return (matrix * lax.rsqrt(jnp.sum(matrix * matrix, -1, keepdims=True) + 1e-06)).astype(BF16)


def unit_pair(matrix, width):
    return jnp.concatenate([unit(matrix[:, :width]), unit(matrix[:, width:])], 1)


def dot(a, b):
    return jnp.dot(a, b, preferred_element_type=F32)


def state_kernel(
    width,
    tok_hbm,
    wk_hbm,
    wv_hbm,
    wq_hbm,
    k_ref,
    v_ref,
    tok,
    wq,
    own,
    one,
    two,
    three,
    weights,
    slices,
    sums,
    sems,
):
    depth = tok.shape[1]
    pair = 2 * width
    part = width // QUARTERS
    chunks = 3
    chunk = depth // chunks
    count = 0

    def copy(source, target):
        nonlocal count
        count += 1
        return pltpu.make_async_copy(source, target, sems.at[count - 1])

    def columns(start, size):
        return pl.ds(start * pair, size * pair)

    first = []
    for i in range(chunks):
        rows = pl.ds(i * chunk, chunk)
        first.append(copy(tok_hbm.at[:, rows], tok.at[:, rows]))
        first.append(copy(wk_hbm.at[rows, columns(0, 2)], weights.at[0, rows]))
    second = [
        copy(wk_hbm.at[:, columns(2, 1)], weights.at[1, :, columns(0, 1)]),
        copy(wv_hbm.at[:, columns(0, 1)], weights.at[1, :, columns(1, 1)]),
    ]
    third = copy(wv_hbm.at[:, columns(1, 2)], weights.at[2])
    last = copy(wq_hbm, wq)
    for item in (*first, *second, third, last):
        item.start()

    def finish_keys(j, product):
        k_ref[:, j * pair : (j + 1) * pair] = unit_pair(product, width)

    def finish_values(j, product):
        here = slice(j * pair, (j + 1) * pair)
        values = product.astype(BF16)
        v_ref[:, here] = values
        both = lax.dot_general(
            k_ref[:, here], values, (((0,), (0,)), ((), ())), preferred_element_type=F32
        )
        for side in range(2):
            head = 2 * j + side
            state = both[side * width : (side + 1) * width, side * width : (side + 1) * width]
            for q in range(QUARTERS):
                slices[q, head * part : (head + 1) * part, :] = state[
                    q * part : (q + 1) * part
                ].astype(BF16)

    for i in range(chunks):
        first[2 * i].wait()
        first[2 * i + 1].wait()
        rows = slice(i * chunk, (i + 1) * chunk)
        product = dot(tok[:, rows], weights[0, rows])
        sums[0] = product if i == 0 else sums[0] + product
    for item in second:
        item.wait()
    sums[1] = dot(tok[...], weights[1])
    finish_keys(0, sums[0, :, :pair])
    finish_keys(1, sums[0, :, pair:])
    third.wait()
    sums[0] = dot(tok[...], weights[2])
    finish_keys(2, sums[1, :, :pair])
    finish_values(0, sums[1, :, pair:])
    finish_values(1, sums[0, :, :pair])
    finish_values(2, sums[0, :, pair:])
    y = lax.axis_index("grp") % QUARTERS
    for distance, target in enumerate((own, one, two, three)):
        target[...] = slices[y ^ distance]
    last.wait()


def states_of(tokens, w_key, w_value, w_query, heads, width):
    rows, depth = tokens.shape
    inner = heads * width
    piece = jax.ShapeDtypeStruct((inner // QUARTERS, width), BF16)
    side = jax.ShapeDtypeStruct((rows, inner), BF16)
    whole = [jax.ShapeDtypeStruct(a.shape, a.dtype) for a in (tokens, w_query)]
    operands = (tokens, w_key, w_value, w_query)
    return pl.pallas_call(
        functools.partial(state_kernel, width),
        out_shape=(side, side, *whole, piece, piece, piece, piece),
        in_specs=[HBM] * 4,
        out_specs=[VMEM] * 8,
        scratch_shapes=[
            pltpu.VMEM((3, depth, 4 * width), BF16),
            pltpu.VMEM((QUARTERS, inner // QUARTERS, width), BF16),
            pltpu.VMEM((2, rows, 4 * width), F32),
            pltpu.SemaphoreType.DMA((10,)),
        ],
        compiler_params=pltpu.CompilerParams(vmem_limit_bytes=24 << 20),
        name="states",
    )(*(pltpu.with_memory_space_constraint(operand, pltpu.HBM) for operand in operands))


def position():
    member = lax.axis_index("grp")
    group = lax.axis_index("seq")
    return member % 4, member // 4, group % 2, group // 2


def bit(index, level):
    return ((index >> level) & 1).astype(F32)


def query_kernel(width, tok, wq, q_ref):
    pair = 2 * width
    for j in range(wq.shape[1] // pair):
        columns = slice(j * pair, (j + 1) * pair)
        q_ref[:, columns] = unit_pair(dot(tok[...], wq[:, columns]), width)


def query_of(tok, wq, width):
    return pl.pallas_call(
        functools.partial(query_kernel, width),
        out_shape=jax.ShapeDtypeStruct((tok.shape[0], wq.shape[1]), BF16),
        in_specs=[VMEM, VMEM],
        out_specs=VMEM,
        compiler_params=pltpu.CompilerParams(vmem_limit_bytes=12 << 20),
        name="query",
    )(tok, wq)


def inside_kernel(width, first, q_ref, k_ref, v_ref, levels, after, inside_ref):
    rows, columns_here = inside_ref.shape
    block = rows // 2
    low = lax.broadcasted_iota(jnp.int32, (block, block), 0) >= lax.broadcasted_iota(
        jnp.int32, (block, block), 1
    )
    for local in range(columns_here // width):
        head = first + local
        columns = slice(head * width, (head + 1) * width)
        scale = levels[0, head]
        for i in range(2):
            here = slice(i * block, (i + 1) * block)
            q = q_ref[here, columns]

            def weigh(keys, masked):
                scores = lax.dot_general(
                    q, keys, (((1,), (1,)), ((), ())), preferred_element_type=F32
                )
                if masked:
                    scores = jnp.where(low, scores, 0.0)
                return (scores * scale).astype(BF16)

            out = dot(weigh(k_ref[here, columns], True), v_ref[here, columns])
            if i:
                out = out + dot(weigh(k_ref[:block, columns], False), v_ref[:block, columns])
            inside_ref[here, local * width : (local + 1) * width] = out


def inside_of(query, keys, values, level_weights, after, first, count, width):
    return pl.pallas_call(
        functools.partial(inside_kernel, width, first),
        out_shape=jax.ShapeDtypeStruct((query.shape[0], count * width), F32),
        in_specs=[VMEM, VMEM, VMEM, SMEM, ANY],
        out_specs=VMEM,
        compiler_params=pltpu.CompilerParams(vmem_limit_bytes=12 << 20),
        name="inside",
    )(query, keys, values, level_weights, after)


def gather_kernel(levels, *refs):
    near = refs[:4]
    x1, x2, x3, mine, z1, z2, z3, local_ref, last_ref = refs[4:]
    y, x, core, z = position()
    heads = levels.shape[1]
    part = mine.shape[0] // heads
    for head in range(heads):
        rows = slice(head * part, (head + 1) * part)

        def factor(level, present):
            return levels[level + 1, head] * (present * 2.0 ** (-0.5 * level))

        def read(ref):
            return ref[rows, :].astype(F32)

        far = (
            factor(2, bit(x, 0)) * x1[1, rows, :].astype(F32)
            + factor(3, bit(x, 1)) * (x2[1, rows, :].astype(F32) + read(x3))
            + factor(4, bit(core ^ 1, 0)) * read(mine)
            + factor(5, bit(z, 0)) * read(z1)
            + factor(6, bit(z, 1)) * (read(z2) + read(z3))
        )
        sides = [read(ref) for ref in near]
        for distance in range(4):
            target = y ^ distance
            local_ref[distance, rows, :] = (
                far
                + factor(0, bit(target, 0)) * sides[distance ^ 1]
                + factor(1, bit(target, 1)) * (sides[distance ^ 2] + sides[distance ^ 3])
            )
        last_ref[rows, :] = jnp.full((part, last_ref.shape[1]), factor(7, bit(z, 2)), F32)


def gather_of(level_weights, near, others):
    shape = near[0].shape
    return pl.pallas_call(
        gather_kernel,
        out_shape=(jax.ShapeDtypeStruct((4, *shape), F32), jax.ShapeDtypeStruct(shape, F32)),
        in_specs=[SMEM] + [VMEM] * 11,
        out_specs=[VMEM, VMEM],
        compiler_params=pltpu.CompilerParams(vmem_limit_bytes=4 << 20),
        name="gather",
    )(level_weights, *near, *others)


def mix_kernel(
    width, q_ref, low_ref, high_ref, own, one, two, three, wo, out_hbm, slices, attended, out, sems
):
    rows, inner = q_ref.shape
    part = width // QUARTERS
    pair = 2 * width
    y = lax.axis_index("grp") % QUARTERS
    for distance, source in enumerate((own, one, two, three)):
        slices[y ^ distance] = source[...]
    half = inner // 2
    zero = jnp.zeros((width, width), BF16)
    pairs = inner // pair

    def states(j):
        halves = []
        for side in range(2):
            head = 2 * j + side
            state = jnp.concatenate(
                [slices[q, head * part : (head + 1) * part, :] for q in range(QUARTERS)], 0
            )
            halves.append(jnp.concatenate([zero, state] if side else [state, zero], 1))
        return jnp.concatenate(halves, 0)

    def inside(here, start):
        ref, start = (low_ref, start) if start < half else (high_ref, start - half)
        return ref[here, start : start + width]

    blocks = 2
    height = rows // blocks
    steps = sems.shape[0] // blocks
    block = out.shape[1] // steps
    copies = []

    def attend(i):
        here = slice(i * height, (i + 1) * height)
        for j in range(pairs):
            columns = slice(j * pair, (j + 1) * pair)
            within = jnp.concatenate(
                [inside(here, j * pair), inside(here, j * pair + width)], 1
            )
            attended[here, columns] = (within + dot(q_ref[here, columns], states(j))).astype(BF16)

    def project(i):
        here = pl.ds(i * height, height)
        for step in range(steps):
            columns = pl.ds(step * block, block)
            out[here, columns] = dot(attended[here, :], wo[:, columns]).astype(BF16)
            copy = pltpu.make_async_copy(
                out.at[here, columns], out_hbm.at[here, columns], sems.at[len(copies)]
            )
            copy.start()
            copies.append(copy)

    attend(0)
    for i in range(blocks):
        if i + 1 < blocks:
            attend(i + 1)
        project(i)
    for copy in copies:
        copy.wait()


def mixed_of(query, insides, pieces, w_output, width):
    rows, inner = query.shape
    wide = w_output.shape[1]
    return pl.pallas_call(
        functools.partial(mix_kernel, width),
        out_shape=jax.ShapeDtypeStruct((rows, wide), BF16),
        in_specs=[VMEM] * 8,
        out_specs=HBM,
        scratch_shapes=[
            pltpu.VMEM((QUARTERS, inner // QUARTERS, width), BF16),
            pltpu.VMEM((rows, inner), BF16),
            pltpu.VMEM((rows, wide), BF16),
            pltpu.SemaphoreType.DMA((6,)),
        ],
        compiler_params=pltpu.CompilerParams(vmem_limit_bytes=16 << 20),
        name="mix",
    )(query, *insides, *pieces, w_output)


AXES = ("seq", "grp")
CORE, Y, X, Z = 16, 1, 4, 32


def flip(value, mask):
    devices = lax.axis_size("seq") * lax.axis_size("grp")
    return lax.ppermute(value, AXES, [(source, source ^ mask) for source in range(devices)])


def plus(total, others):
    for other in others:
        total = total + other.astype(F32)
    return total


def per_device(tokens, w_query, w_key, w_value, w_output, level_weights):
    heads = level_weights.shape[1]
    width = w_query.shape[1] // heads
    half = heads // 2
    keys, values, tok, wq, *sent = states_of(tokens, w_key, w_value, w_query, heads, width)
    n3, n2, n1, n0 = (
        flip(sent[3], CORE | 3 * Y),
        flip(sent[2], CORE | 2 * Y),
        flip(sent[1], CORE | Y),
        flip(sent[0], CORE),
    )
    query = query_of(tok, wq, width)
    n3, n2, n1, n0, query = lax.optimization_barrier((n3, n2, n1, n0, query))
    near = (n0, n1, n2, n3)
    total = plus(n0.astype(F32), near[1:])
    going = total.astype(BF16)

    own = flip(going, CORE)
    x3 = flip(going, CORE | 3 * X)
    both = jnp.stack([going, own])
    x2, x1 = flip(both, CORE | 2 * X), flip(both, CORE | X)
    other3 = flip(x3, CORE)
    low = inside_of(query, keys, values, level_weights, x3, 0, half, width)
    other3, x2, x1, low = lax.optimization_barrier((other3, x2, x1, low))
    mine = plus(own.astype(F32), (x1[0], x2[0], x3))
    total = plus(total + mine, (x1[1], x2[1], other3))
    mine = mine.astype(BF16)
    going = total.astype(BF16)
    z1, z3, z2 = (flip(going, CORE | distance * Z) for distance in (1, 3, 2))
    high = inside_of(query, keys, values, level_weights, going, half, half, width)
    z1, z3, z2, high = lax.optimization_barrier((z1, z3, z2, high))
    going = plus(total, (z3, z2, z1)).astype(BF16)

    past = flip(going, CORE | 6 * Z)
    gathered, factor = gather_of(level_weights, near, (x1, x2, other3, mine, z1, z2, z3))
    past, gathered, factor = lax.optimization_barrier((past, gathered, factor))
    last = factor * past.astype(F32)
    back = [(gathered[distance] + last).astype(BF16) for distance in range(4)]
    p3, p2, p1, p0 = lax.optimization_barrier(
        (
            flip(back[3], CORE | 3 * Y),
            flip(back[2], CORE | 2 * Y),
            flip(back[1], CORE | Y),
            flip(back[0], CORE),
        )
    )
    return mixed_of(query, (low, high), (p0, p1, p2, p3), w_output, width)


def solution(mesh):
    placed = (P(("seq", "grp"), None), P(), P(), P(), P(), P())
    return jax.shard_map(
        per_device, mesh=mesh, in_specs=placed, out_specs=P(("seq", "grp"), None), check_vma=False
    )
```

```python
import functools

import jax
import jax.numpy as jnp
from jax import lax
from jax.experimental import pallas as pl
from jax.experimental.pallas import tpu as pltpu
from jax.sharding import PartitionSpec as P

BF16 = jnp.bfloat16
F32 = jnp.float32
VMEM = pl.BlockSpec(memory_space=pltpu.VMEM)
SMEM = pl.BlockSpec(memory_space=pltpu.SMEM)
ANY = pl.BlockSpec(memory_space=pl.ANY)
HBM = pl.BlockSpec(memory_space=pltpu.HBM)
QUARTERS = 4


def unit(matrix):
    return (matrix * lax.rsqrt(jnp.sum(matrix * matrix, -1, keepdims=True) + 1e-06)).astype(BF16)


def unit_pair(matrix, width):
    return jnp.concatenate([unit(matrix[:, :width]), unit(matrix[:, width:])], 1)


def dot(a, b):
    return jnp.dot(a, b, preferred_element_type=F32)


def state_kernel(
    width,
    tok_hbm,
    wk_hbm,
    wv_hbm,
    wq_hbm,
    k_ref,
    v_ref,
    tok,
    wq,
    own,
    one,
    two,
    three,
    weights,
    slices,
    sums,
    sems,
):
    depth = tok.shape[1]
    pair = 2 * width
    part = width // QUARTERS
    chunks = 3
    chunk = depth // chunks
    count = 0

    def copy(source, target):
        nonlocal count
        count += 1
        return pltpu.make_async_copy(source, target, sems.at[count - 1])

    def columns(start, size):
        return pl.ds(start * pair, size * pair)

    first = []
    for i in range(chunks):
        rows = pl.ds(i * chunk, chunk)
        first.append(copy(tok_hbm.at[:, rows], tok.at[:, rows]))
        first.append(copy(wk_hbm.at[rows, columns(0, 2)], weights.at[0, rows]))
    second = [
        copy(wk_hbm.at[:, columns(2, 1)], weights.at[1, :, columns(0, 1)]),
        copy(wv_hbm.at[:, columns(0, 1)], weights.at[1, :, columns(1, 1)]),
    ]
    third = copy(wv_hbm.at[:, columns(1, 2)], weights.at[2])
    last = copy(wq_hbm, wq)
    for item in (*first, *second, third, last):
        item.start()

    def finish_keys(j, product):
        k_ref[:, j * pair : (j + 1) * pair] = unit_pair(product, width)

    def finish_values(j, product):
        here = slice(j * pair, (j + 1) * pair)
        values = product.astype(BF16)
        v_ref[:, here] = values
        both = lax.dot_general(
            k_ref[:, here], values, (((0,), (0,)), ((), ())), preferred_element_type=F32
        )
        for side in range(2):
            head = 2 * j + side
            state = both[side * width : (side + 1) * width, side * width : (side + 1) * width]
            for q in range(QUARTERS):
                slices[q, head * part : (head + 1) * part, :] = state[
                    q * part : (q + 1) * part
                ].astype(BF16)

    for i in range(chunks):
        first[2 * i].wait()
        first[2 * i + 1].wait()
        rows = slice(i * chunk, (i + 1) * chunk)
        product = dot(tok[:, rows], weights[0, rows])
        sums[0] = product if i == 0 else sums[0] + product
    for item in second:
        item.wait()
    sums[1] = dot(tok[...], weights[1])
    finish_keys(0, sums[0, :, :pair])
    finish_keys(1, sums[0, :, pair:])
    third.wait()
    sums[0] = dot(tok[...], weights[2])
    finish_keys(2, sums[1, :, :pair])
    finish_values(0, sums[1, :, pair:])
    finish_values(1, sums[0, :, :pair])
    finish_values(2, sums[0, :, pair:])
    y = lax.axis_index("grp") % QUARTERS
    for distance, target in enumerate((own, one, two, three)):
        target[...] = slices[y ^ distance]
    last.wait()


def states_of(tokens, w_key, w_value, w_query, heads, width):
    rows, depth = tokens.shape
    inner = heads * width
    piece = jax.ShapeDtypeStruct((inner // QUARTERS, width), BF16)
    side = jax.ShapeDtypeStruct((rows, inner), BF16)
    whole = [jax.ShapeDtypeStruct(a.shape, a.dtype) for a in (tokens, w_query)]
    operands = (tokens, w_key, w_value, w_query)
    return pl.pallas_call(
        functools.partial(state_kernel, width),
        out_shape=(side, side, *whole, piece, piece, piece, piece),
        in_specs=[HBM] * 4,
        out_specs=[VMEM] * 8,
        scratch_shapes=[
            pltpu.VMEM((3, depth, 4 * width), BF16),
            pltpu.VMEM((QUARTERS, inner // QUARTERS, width), BF16),
            pltpu.VMEM((2, rows, 4 * width), F32),
            pltpu.SemaphoreType.DMA((10,)),
        ],
        compiler_params=pltpu.CompilerParams(vmem_limit_bytes=24 << 20),
        name="states",
    )(*(pltpu.with_memory_space_constraint(operand, pltpu.HBM) for operand in operands))


def position():
    member = lax.axis_index("grp")
    group = lax.axis_index("seq")
    return member % 4, member // 4, group % 2, group // 2


def bit(index, level):
    return ((index >> level) & 1).astype(F32)


def query_kernel(width, tok, wq, q_ref):
    pair = 2 * width
    for j in range(wq.shape[1] // pair):
        columns = slice(j * pair, (j + 1) * pair)
        q_ref[:, columns] = unit_pair(dot(tok[...], wq[:, columns]), width)


def query_of(tok, wq, width):
    return pl.pallas_call(
        functools.partial(query_kernel, width),
        out_shape=jax.ShapeDtypeStruct((tok.shape[0], wq.shape[1]), BF16),
        in_specs=[VMEM, VMEM],
        out_specs=VMEM,
        compiler_params=pltpu.CompilerParams(vmem_limit_bytes=12 << 20),
        name="query",
    )(tok, wq)


def inside_kernel(width, first, q_ref, k_ref, v_ref, levels, after, inside_ref):
    rows, columns_here = inside_ref.shape
    block = rows // 2
    low = lax.broadcasted_iota(jnp.int32, (block, block), 0) >= lax.broadcasted_iota(
        jnp.int32, (block, block), 1
    )
    for local in range(columns_here // width):
        head = first + local
        columns = slice(head * width, (head + 1) * width)
        scale = levels[0, head]
        for i in range(2):
            here = slice(i * block, (i + 1) * block)
            q = q_ref[here, columns]

            def weigh(keys, masked):
                scores = lax.dot_general(
                    q, keys, (((1,), (1,)), ((), ())), preferred_element_type=F32
                )
                if masked:
                    scores = jnp.where(low, scores, 0.0)
                return (scores * scale).astype(BF16)

            out = dot(weigh(k_ref[here, columns], True), v_ref[here, columns])
            if i:
                out = out + dot(weigh(k_ref[:block, columns], False), v_ref[:block, columns])
            inside_ref[here, local * width : (local + 1) * width] = out


def inside_of(query, keys, values, level_weights, after, first, count, width):
    return pl.pallas_call(
        functools.partial(inside_kernel, width, first),
        out_shape=jax.ShapeDtypeStruct((query.shape[0], count * width), F32),
        in_specs=[VMEM, VMEM, VMEM, SMEM, ANY],
        out_specs=VMEM,
        compiler_params=pltpu.CompilerParams(vmem_limit_bytes=12 << 20),
        name="inside",
    )(query, keys, values, level_weights, after)


def gather_kernel(levels, *refs):
    near = refs[:4]
    crossed, mine, z1, z2, z3, other3, local_ref, last_ref = refs[4:]
    y, x, core, z = position()
    heads = levels.shape[1]
    part = mine.shape[0] // heads
    for head in range(heads):
        rows = slice(head * part, (head + 1) * part)

        def factor(level, present):
            return levels[level + 1, head] * (present * 2.0 ** (-0.5 * level))

        def read(ref):
            return ref[rows, :].astype(F32)

        far = (
            factor(2, bit(x, 0)) * crossed[0, rows, :].astype(F32)
            + factor(3, bit(x, 1)) * crossed[1, rows, :].astype(F32)
            + factor(4, bit(core ^ 1, 0)) * read(mine)
            + factor(5, bit(z, 0)) * read(z1)
            + factor(6, bit(z, 1)) * (read(z2) + read(z3) + read(other3))
        )
        sides = [read(ref) for ref in near]
        for distance in range(4):
            target = y ^ distance
            local_ref[distance, rows, :] = (
                far
                + factor(0, bit(target, 0)) * sides[distance ^ 1]
                + factor(1, bit(target, 1)) * (sides[distance ^ 2] + sides[distance ^ 3])
            )
        last_ref[rows, :] = jnp.full((part, last_ref.shape[1]), factor(7, bit(z, 2)), F32)


def gather_of(level_weights, near, others):
    shape = near[0].shape
    return pl.pallas_call(
        gather_kernel,
        out_shape=(jax.ShapeDtypeStruct((4, *shape), F32), jax.ShapeDtypeStruct(shape, F32)),
        in_specs=[SMEM] + [VMEM] * 10,
        out_specs=[VMEM, VMEM],
        compiler_params=pltpu.CompilerParams(vmem_limit_bytes=4 << 20),
        name="gather",
    )(level_weights, *near, *others)


def mix_kernel(
    width, q_ref, low_ref, high_ref, own, one, two, three, wo, out_hbm, slices, attended, out, sems
):
    rows, inner = q_ref.shape
    part = width // QUARTERS
    pair = 2 * width
    y = lax.axis_index("grp") % QUARTERS
    for distance, source in enumerate((own, one, two, three)):
        slices[y ^ distance] = source[...]
    half = inner // 2
    zero = jnp.zeros((width, width), BF16)
    pairs = inner // pair

    def states(j):
        halves = []
        for side in range(2):
            head = 2 * j + side
            state = jnp.concatenate(
                [slices[q, head * part : (head + 1) * part, :] for q in range(QUARTERS)], 0
            )
            halves.append(jnp.concatenate([zero, state] if side else [state, zero], 1))
        return jnp.concatenate(halves, 0)

    def inside(here, start):
        ref, start = (low_ref, start) if start < half else (high_ref, start - half)
        return ref[here, start : start + width]

    blocks = 2
    height = rows // blocks
    steps = sems.shape[0] // blocks
    block = out.shape[1] // steps
    copies = []

    def attend(i):
        here = slice(i * height, (i + 1) * height)
        for j in range(pairs):
            columns = slice(j * pair, (j + 1) * pair)
            within = jnp.concatenate(
                [inside(here, j * pair), inside(here, j * pair + width)], 1
            )
            attended[here, columns] = (within + dot(q_ref[here, columns], states(j))).astype(BF16)

    def project(i):
        here = pl.ds(i * height, height)
        for step in range(steps):
            columns = pl.ds(step * block, block)
            out[here, columns] = dot(attended[here, :], wo[:, columns]).astype(BF16)
            copy = pltpu.make_async_copy(
                out.at[here, columns], out_hbm.at[here, columns], sems.at[len(copies)]
            )
            copy.start()
            copies.append(copy)

    attend(0)
    for i in range(blocks):
        if i + 1 < blocks:
            attend(i + 1)
        project(i)
    for copy in copies:
        copy.wait()


def mixed_of(query, insides, pieces, w_output, width):
    rows, inner = query.shape
    wide = w_output.shape[1]
    return pl.pallas_call(
        functools.partial(mix_kernel, width),
        out_shape=jax.ShapeDtypeStruct((rows, wide), BF16),
        in_specs=[VMEM] * 8,
        out_specs=HBM,
        scratch_shapes=[
            pltpu.VMEM((QUARTERS, inner // QUARTERS, width), BF16),
            pltpu.VMEM((rows, inner), BF16),
            pltpu.VMEM((rows, wide), BF16),
            pltpu.SemaphoreType.DMA((6,)),
        ],
        compiler_params=pltpu.CompilerParams(vmem_limit_bytes=16 << 20),
        name="mix",
    )(query, *insides, *pieces, w_output)


AXES = ("seq", "grp")
CORE, Y, X, Z = 16, 1, 4, 32


def flip(value, mask):
    devices = lax.axis_size("seq") * lax.axis_size("grp")
    return lax.ppermute(value, AXES, [(source, source ^ mask) for source in range(devices)])


def plus(total, others):
    for other in others:
        total = total + other.astype(F32)
    return total


def per_device(tokens, w_query, w_key, w_value, w_output, level_weights):
    heads = level_weights.shape[1]
    width = w_query.shape[1] // heads
    half = heads // 2
    keys, values, tok, wq, *sent = states_of(tokens, w_key, w_value, w_query, heads, width)
    n2, n3, n1, n0 = (
        flip(sent[2], CORE | 2 * Y),
        flip(sent[3], CORE | 3 * Y),
        flip(sent[1], CORE | Y),
        flip(sent[0], CORE),
    )
    query = query_of(tok, wq, width)
    n2, n3, n1, n0, query = lax.optimization_barrier((n2, n3, n1, n0, query))
    near = (n0, n1, n2, n3)
    going = plus(n0.astype(F32), near[1:]).astype(BF16)

    x2, x3, x1 = (flip(going, CORE | distance * X) for distance in (2, 3, 1))
    own = flip(going, CORE)
    low = inside_of(query, keys, values, level_weights, going, 0, half, width)
    x2, x3, x1, own, low = lax.optimization_barrier((x2, x3, x1, own, low))
    total = plus(own.astype(F32), (x1, x2, x3))
    mine = total.astype(BF16)

    other = flip(mine, CORE)
    z3 = flip(mine, CORE | 3 * Z)
    total = plus(total, (other,))
    going = total.astype(BF16)
    z2, z1 = flip(going, CORE | 2 * Z), flip(going, CORE | Z)
    other3 = flip(z3, CORE)
    high = inside_of(query, keys, values, level_weights, going, half, half, width)
    crossing = jnp.stack([x1.astype(F32), plus(x2.astype(F32), (x3,))]).astype(BF16)
    crossing, high = lax.optimization_barrier((crossing, high))
    crossed = flip(crossing, CORE)
    other3, z2, z1, high = lax.optimization_barrier((other3, z2, z1, high))
    going = plus(total, (z3, z2, z1, other3)).astype(BF16)

    past = flip(going, CORE | 6 * Z)
    gathered, factor = gather_of(level_weights, near, (crossed, mine, z1, z2, z3, other3))
    past, gathered, factor = lax.optimization_barrier((past, gathered, factor))
    last = factor * past.astype(F32)
    back = [(gathered[distance] + last).astype(BF16) for distance in range(4)]
    p2, p3, p1, p0 = lax.optimization_barrier(
        (
            flip(back[2], CORE | 2 * Y),
            flip(back[3], CORE | 3 * Y),
            flip(back[1], CORE | Y),
            flip(back[0], CORE),
        )
    )
    return mixed_of(query, (low, high), (p0, p1, p2, p3), w_output, width)


def solution(mesh):
    placed = (P(("seq", "grp"), None), P(), P(), P(), P(), P())
    return jax.shard_map(
        per_device, mesh=mesh, in_specs=placed, out_specs=P(("seq", "grp"), None), check_vma=False
    )
```

```python
import functools

import jax
import jax.numpy as jnp
from jax import lax
from jax.experimental import pallas as pl
from jax.experimental.pallas import tpu as pltpu
from jax.sharding import PartitionSpec as P

BF16 = jnp.bfloat16
F32 = jnp.float32
VMEM = pl.BlockSpec(memory_space=pltpu.VMEM)
SMEM = pl.BlockSpec(memory_space=pltpu.SMEM)
ANY = pl.BlockSpec(memory_space=pl.ANY)
HBM = pl.BlockSpec(memory_space=pltpu.HBM)
QUARTERS = 4


def unit(matrix):
    return (matrix * lax.rsqrt(jnp.sum(matrix * matrix, -1, keepdims=True) + 1e-06)).astype(BF16)


def unit_pair(matrix, width):
    return jnp.concatenate([unit(matrix[:, :width]), unit(matrix[:, width:])], 1)


def dot(a, b):
    return jnp.dot(a, b, preferred_element_type=F32)


def state_kernel(
    width,
    tok_hbm,
    wk_hbm,
    wv_hbm,
    wq_hbm,
    k_ref,
    v_ref,
    tok,
    wq,
    own,
    one,
    two,
    three,
    weights,
    slices,
    sums,
    sems,
):
    depth = tok.shape[1]
    pair = 2 * width
    part = width // QUARTERS
    chunks = 3
    chunk = depth // chunks
    count = 0

    def copy(source, target):
        nonlocal count
        count += 1
        return pltpu.make_async_copy(source, target, sems.at[count - 1])

    def columns(start, size):
        return pl.ds(start * pair, size * pair)

    first = []
    for i in range(chunks):
        rows = pl.ds(i * chunk, chunk)
        first.append(copy(tok_hbm.at[:, rows], tok.at[:, rows]))
        first.append(copy(wk_hbm.at[rows, columns(0, 2)], weights.at[0, rows]))
    second = [
        copy(wk_hbm.at[:, columns(2, 1)], weights.at[1, :, columns(0, 1)]),
        copy(wv_hbm.at[:, columns(0, 1)], weights.at[1, :, columns(1, 1)]),
    ]
    third = copy(wv_hbm.at[:, columns(1, 2)], weights.at[2])
    last = copy(wq_hbm, wq)
    for item in (*first, *second, third, last):
        item.start()

    def finish_keys(j, product):
        k_ref[:, j * pair : (j + 1) * pair] = unit_pair(product, width)

    def finish_values(j, product):
        here = slice(j * pair, (j + 1) * pair)
        values = product.astype(BF16)
        v_ref[:, here] = values
        both = lax.dot_general(
            k_ref[:, here], values, (((0,), (0,)), ((), ())), preferred_element_type=F32
        )
        for side in range(2):
            head = 2 * j + side
            state = both[side * width : (side + 1) * width, side * width : (side + 1) * width]
            for q in range(QUARTERS):
                slices[q, head * part : (head + 1) * part, :] = state[
                    q * part : (q + 1) * part
                ].astype(BF16)

    for i in range(chunks):
        first[2 * i].wait()
        first[2 * i + 1].wait()
        rows = slice(i * chunk, (i + 1) * chunk)
        product = dot(tok[:, rows], weights[0, rows])
        sums[0] = product if i == 0 else sums[0] + product
    for item in second:
        item.wait()
    sums[1] = dot(tok[...], weights[1])
    finish_keys(0, sums[0, :, :pair])
    finish_keys(1, sums[0, :, pair:])
    third.wait()
    sums[0] = dot(tok[...], weights[2])
    finish_keys(2, sums[1, :, :pair])
    finish_values(0, sums[1, :, pair:])
    finish_values(1, sums[0, :, :pair])
    finish_values(2, sums[0, :, pair:])
    y = lax.axis_index("grp") % QUARTERS
    for distance, target in enumerate((own, one, two, three)):
        target[...] = slices[y ^ distance]
    last.wait()


def states_of(tokens, w_key, w_value, w_query, heads, width):
    rows, depth = tokens.shape
    inner = heads * width
    piece = jax.ShapeDtypeStruct((inner // QUARTERS, width), BF16)
    side = jax.ShapeDtypeStruct((rows, inner), BF16)
    whole = [jax.ShapeDtypeStruct(a.shape, a.dtype) for a in (tokens, w_query)]
    operands = (tokens, w_key, w_value, w_query)
    return pl.pallas_call(
        functools.partial(state_kernel, width),
        out_shape=(side, side, *whole, piece, piece, piece, piece),
        in_specs=[HBM] * 4,
        out_specs=[VMEM] * 8,
        scratch_shapes=[
            pltpu.VMEM((3, depth, 4 * width), BF16),
            pltpu.VMEM((QUARTERS, inner // QUARTERS, width), BF16),
            pltpu.VMEM((2, rows, 4 * width), F32),
            pltpu.SemaphoreType.DMA((10,)),
        ],
        compiler_params=pltpu.CompilerParams(vmem_limit_bytes=24 << 20),
        name="states",
    )(*(pltpu.with_memory_space_constraint(operand, pltpu.HBM) for operand in operands))


def position():
    member = lax.axis_index("grp")
    group = lax.axis_index("seq")
    return member % 4, member // 4, group % 2, group // 2


def bit(index, level):
    return ((index >> level) & 1).astype(F32)


def query_kernel(width, tok, wq, q_ref):
    pair = 2 * width
    for j in range(wq.shape[1] // pair):
        columns = slice(j * pair, (j + 1) * pair)
        q_ref[:, columns] = unit_pair(dot(tok[...], wq[:, columns]), width)


def query_of(tok, wq, width):
    return pl.pallas_call(
        functools.partial(query_kernel, width),
        out_shape=jax.ShapeDtypeStruct((tok.shape[0], wq.shape[1]), BF16),
        in_specs=[VMEM, VMEM],
        out_specs=VMEM,
        compiler_params=pltpu.CompilerParams(vmem_limit_bytes=12 << 20),
        name="query",
    )(tok, wq)


def inside_kernel(width, first, q_ref, k_ref, v_ref, levels, after, inside_ref):
    rows, columns_here = inside_ref.shape
    block = rows // 2
    low = lax.broadcasted_iota(jnp.int32, (block, block), 0) >= lax.broadcasted_iota(
        jnp.int32, (block, block), 1
    )
    for local in range(columns_here // width):
        head = first + local
        columns = slice(head * width, (head + 1) * width)
        scale = levels[0, head]
        for i in range(2):
            here = slice(i * block, (i + 1) * block)
            q = q_ref[here, columns]

            def weigh(keys, masked):
                scores = lax.dot_general(
                    q, keys, (((1,), (1,)), ((), ())), preferred_element_type=F32
                )
                if masked:
                    scores = jnp.where(low, scores, 0.0)
                return (scores * scale).astype(BF16)

            out = dot(weigh(k_ref[here, columns], True), v_ref[here, columns])
            if i:
                out = out + dot(weigh(k_ref[:block, columns], False), v_ref[:block, columns])
            inside_ref[here, local * width : (local + 1) * width] = out


def inside_of(query, keys, values, level_weights, after, first, count, width):
    return pl.pallas_call(
        functools.partial(inside_kernel, width, first),
        out_shape=jax.ShapeDtypeStruct((query.shape[0], count * width), F32),
        in_specs=[VMEM, VMEM, VMEM, SMEM, ANY],
        out_specs=VMEM,
        compiler_params=pltpu.CompilerParams(vmem_limit_bytes=12 << 20),
        name="inside",
    )(query, keys, values, level_weights, after)


def gather_kernel(levels, *refs):
    near = refs[:4]
    crossed, mine, z1, z2, z3, other3, local_ref, last_ref = refs[4:]
    y, x, core, z = position()
    heads = levels.shape[1]
    part = mine.shape[0] // heads
    for head in range(heads):
        rows = slice(head * part, (head + 1) * part)

        def factor(level, present):
            return levels[level + 1, head] * (present * 2.0 ** (-0.5 * level))

        def read(ref):
            return ref[rows, :].astype(F32)

        far = (
            factor(2, bit(x, 0)) * crossed[0, rows, :].astype(F32)
            + factor(3, bit(x, 1)) * crossed[1, rows, :].astype(F32)
            + factor(4, bit(core ^ 1, 0)) * read(mine)
            + factor(5, bit(z, 0)) * read(z1)
            + factor(6, bit(z, 1)) * (read(z2) + read(z3) + read(other3))
        )
        sides = [read(ref) for ref in near]
        for distance in range(4):
            target = y ^ distance
            local_ref[distance, rows, :] = (
                far
                + factor(0, bit(target, 0)) * sides[distance ^ 1]
                + factor(1, bit(target, 1)) * (sides[distance ^ 2] + sides[distance ^ 3])
            )
        last_ref[rows, :] = jnp.full((part, last_ref.shape[1]), factor(7, bit(z, 2)), F32)


def gather_of(level_weights, near, others):
    shape = near[0].shape
    return pl.pallas_call(
        gather_kernel,
        out_shape=(jax.ShapeDtypeStruct((4, *shape), F32), jax.ShapeDtypeStruct(shape, F32)),
        in_specs=[SMEM] + [VMEM] * 10,
        out_specs=[VMEM, VMEM],
        compiler_params=pltpu.CompilerParams(vmem_limit_bytes=4 << 20),
        name="gather",
    )(level_weights, *near, *others)


def mix_kernel(
    width, q_ref, *refs
):
    insides = refs[:3]
    own, one, two, three, wo, out_hbm, slices, attended, out, sems = refs[3:]
    rows, inner = q_ref.shape
    part = width // QUARTERS
    pair = 2 * width
    y = lax.axis_index("grp") % QUARTERS
    for distance, source in enumerate((own, one, two, three)):
        slices[y ^ distance] = source[...]
    zero = jnp.zeros((width, width), BF16)
    pairs = inner // pair

    def states(j):
        halves = []
        for side in range(2):
            head = 2 * j + side
            state = jnp.concatenate(
                [slices[q, head * part : (head + 1) * part, :] for q in range(QUARTERS)], 0
            )
            halves.append(jnp.concatenate([zero, state] if side else [state, zero], 1))
        return jnp.concatenate(halves, 0)

    blocks = 2
    height = rows // blocks
    steps = sems.shape[0] // blocks
    block = out.shape[1] // steps
    copies = []

    def attend(i):
        here = slice(i * height, (i + 1) * height)
        for j in range(pairs):
            columns = slice(j * pair, (j + 1) * pair)
            attended[here, columns] = (
                insides[j][here, :] + dot(q_ref[here, columns], states(j))
            ).astype(BF16)

    def project(i):
        here = pl.ds(i * height, height)
        for step in range(steps):
            columns = pl.ds(step * block, block)
            out[here, columns] = dot(attended[here, :], wo[:, columns]).astype(BF16)
            copy = pltpu.make_async_copy(
                out.at[here, columns], out_hbm.at[here, columns], sems.at[len(copies)]
            )
            copy.start()
            copies.append(copy)

    attend(0)
    for i in range(blocks):
        if i + 1 < blocks:
            attend(i + 1)
        project(i)
    for copy in copies:
        copy.wait()


def mixed_of(query, insides, pieces, w_output, width):
    rows, inner = query.shape
    wide = w_output.shape[1]
    return pl.pallas_call(
        functools.partial(mix_kernel, width),
        out_shape=jax.ShapeDtypeStruct((rows, wide), BF16),
        in_specs=[VMEM] * 9,
        out_specs=HBM,
        scratch_shapes=[
            pltpu.VMEM((QUARTERS, inner // QUARTERS, width), BF16),
            pltpu.VMEM((rows, inner), BF16),
            pltpu.VMEM((rows, wide), BF16),
            pltpu.SemaphoreType.DMA((6,)),
        ],
        compiler_params=pltpu.CompilerParams(vmem_limit_bytes=16 << 20),
        name="mix",
    )(query, *insides, *pieces, w_output)


AXES = ("seq", "grp")
CORE, Y, X, Z = 16, 1, 4, 32


def flip(value, mask):
    devices = lax.axis_size("seq") * lax.axis_size("grp")
    return lax.ppermute(value, AXES, [(source, source ^ mask) for source in range(devices)])


def plus(total, others):
    for other in others:
        total = total + other.astype(F32)
    return total


def per_device(tokens, w_query, w_key, w_value, w_output, level_weights):
    heads = level_weights.shape[1]
    width = w_query.shape[1] // heads
    keys, values, tok, wq, *sent = states_of(tokens, w_key, w_value, w_query, heads, width)
    n2, n3, n1, n0 = (
        flip(sent[2], CORE | 2 * Y),
        flip(sent[3], CORE | 3 * Y),
        flip(sent[1], CORE | Y),
        flip(sent[0], CORE),
    )
    query = query_of(tok, wq, width)
    n2, n3, n1, n0, query = lax.optimization_barrier((n2, n3, n1, n0, query))
    near = (n0, n1, n2, n3)
    going = plus(n0.astype(F32), near[1:]).astype(BF16)

    x2, x3, x1 = (flip(going, CORE | distance * X) for distance in (2, 3, 1))
    own = flip(going, CORE)
    inside0 = inside_of(query, keys, values, level_weights, going, 0, 2, width)
    x2, x3, x1, own, inside0 = lax.optimization_barrier((x2, x3, x1, own, inside0))
    total = plus(own.astype(F32), (x1, x2, x3))
    mine = total.astype(BF16)

    other = flip(mine, CORE)
    z3 = flip(mine, CORE | 3 * Z)
    total = plus(total, (other,))
    going = total.astype(BF16)
    z2, z1 = flip(going, CORE | 2 * Z), flip(going, CORE | Z)
    other3 = flip(z3, CORE)
    inside1 = inside_of(query, keys, values, level_weights, going, 2, 2, width)
    crossing = jnp.stack([x1.astype(F32), plus(x2.astype(F32), (x3,))]).astype(BF16)
    crossing, inside1 = lax.optimization_barrier((crossing, inside1))
    crossed = flip(crossing, CORE)
    other3, z2, z1, inside1 = lax.optimization_barrier((other3, z2, z1, inside1))
    going = plus(total, (z3, z2, z1, other3)).astype(BF16)

    past = flip(going, CORE | 6 * Z)
    gathered, factor = gather_of(level_weights, near, (crossed, mine, z1, z2, z3, other3))
    past, gathered, factor = lax.optimization_barrier((past, gathered, factor))
    last = factor * past.astype(F32)
    back = [(gathered[distance] + last).astype(BF16) for distance in range(4)]
    p2, p3, p1, p0 = (
        flip(back[2], CORE | 2 * Y),
        flip(back[3], CORE | 3 * Y),
        flip(back[1], CORE | Y),
        flip(back[0], CORE),
    )
    inside2 = inside_of(query, keys, values, level_weights, back[0], 4, 2, width)
    p2, p3, p1, p0, inside2 = lax.optimization_barrier((p2, p3, p1, p0, inside2))
    return mixed_of(query, (inside0, inside1, inside2), (p0, p1, p2, p3), w_output, width)


def solution(mesh):
    placed = (P(("seq", "grp"), None), P(), P(), P(), P(), P())
    return jax.shard_map(
        per_device, mesh=mesh, in_specs=placed, out_specs=P(("seq", "grp"), None), check_vma=False
    )
```

```python
import functools

import jax
import jax.numpy as jnp
from jax import lax
from jax.experimental import pallas as pl
from jax.experimental.pallas import tpu as pltpu
from jax.sharding import PartitionSpec as P

BF16 = jnp.bfloat16
F32 = jnp.float32
VMEM = pl.BlockSpec(memory_space=pltpu.VMEM)
SMEM = pl.BlockSpec(memory_space=pltpu.SMEM)
ANY = pl.BlockSpec(memory_space=pl.ANY)
HBM = pl.BlockSpec(memory_space=pltpu.HBM)
QUARTERS = 4


def unit(matrix):
    return (matrix * lax.rsqrt(jnp.sum(matrix * matrix, -1, keepdims=True) + 1e-06)).astype(BF16)


def unit_pair(matrix, width):
    return jnp.concatenate([unit(matrix[:, :width]), unit(matrix[:, width:])], 1)


def dot(a, b):
    return jnp.dot(a, b, preferred_element_type=F32)


def state_kernel(
    width,
    tok_hbm,
    wk_hbm,
    wv_hbm,
    wq_hbm,
    k_ref,
    v_ref,
    tok,
    wq,
    own,
    one,
    two,
    three,
    weights,
    slices,
    sums,
    sems,
):
    depth = tok.shape[1]
    pair = 2 * width
    part = width // QUARTERS
    chunks = 3
    chunk = depth // chunks
    count = 0

    def copy(source, target):
        nonlocal count
        count += 1
        return pltpu.make_async_copy(source, target, sems.at[count - 1])

    def columns(start, size):
        return pl.ds(start * pair, size * pair)

    first = []
    for i in range(chunks):
        rows = pl.ds(i * chunk, chunk)
        first.append(copy(tok_hbm.at[:, rows], tok.at[:, rows]))
        first.append(copy(wk_hbm.at[rows, columns(0, 2)], weights.at[0, rows]))
    second = [
        copy(wk_hbm.at[:, columns(2, 1)], weights.at[1, :, columns(0, 1)]),
        copy(wv_hbm.at[:, columns(0, 1)], weights.at[1, :, columns(1, 1)]),
    ]
    third = copy(wv_hbm.at[:, columns(1, 2)], weights.at[2])
    last = copy(wq_hbm, wq)
    for item in (*first, *second, third, last):
        item.start()

    def finish_keys(j, product):
        k_ref[:, j * pair : (j + 1) * pair] = unit_pair(product, width)

    def finish_values(j, product):
        here = slice(j * pair, (j + 1) * pair)
        values = product.astype(BF16)
        v_ref[:, here] = values
        both = lax.dot_general(
            k_ref[:, here], values, (((0,), (0,)), ((), ())), preferred_element_type=F32
        )
        for side in range(2):
            head = 2 * j + side
            state = both[side * width : (side + 1) * width, side * width : (side + 1) * width]
            for q in range(QUARTERS):
                slices[q, head * part : (head + 1) * part, :] = state[
                    q * part : (q + 1) * part
                ].astype(BF16)

    for i in range(chunks):
        first[2 * i].wait()
        first[2 * i + 1].wait()
        rows = slice(i * chunk, (i + 1) * chunk)
        product = dot(tok[:, rows], weights[0, rows])
        sums[0] = product if i == 0 else sums[0] + product
    for item in second:
        item.wait()
    sums[1] = dot(tok[...], weights[1])
    finish_keys(0, sums[0, :, :pair])
    finish_keys(1, sums[0, :, pair:])
    third.wait()
    sums[0] = dot(tok[...], weights[2])
    finish_keys(2, sums[1, :, :pair])
    finish_values(0, sums[1, :, pair:])
    finish_values(1, sums[0, :, :pair])
    finish_values(2, sums[0, :, pair:])
    y = lax.axis_index("grp") % QUARTERS
    for distance, target in enumerate((own, one, two, three)):
        target[...] = slices[y ^ distance]
    last.wait()


def states_of(tokens, w_key, w_value, w_query, heads, width):
    rows, depth = tokens.shape
    inner = heads * width
    piece = jax.ShapeDtypeStruct((inner // QUARTERS, width), BF16)
    side = jax.ShapeDtypeStruct((rows, inner), BF16)
    whole = [jax.ShapeDtypeStruct(a.shape, a.dtype) for a in (tokens, w_query)]
    operands = (tokens, w_key, w_value, w_query)
    return pl.pallas_call(
        functools.partial(state_kernel, width),
        out_shape=(side, side, *whole, piece, piece, piece, piece),
        in_specs=[HBM] * 4,
        out_specs=[VMEM] * 8,
        scratch_shapes=[
            pltpu.VMEM((3, depth, 4 * width), BF16),
            pltpu.VMEM((QUARTERS, inner // QUARTERS, width), BF16),
            pltpu.VMEM((2, rows, 4 * width), F32),
            pltpu.SemaphoreType.DMA((10,)),
        ],
        compiler_params=pltpu.CompilerParams(vmem_limit_bytes=24 << 20),
        name="states",
    )(*(pltpu.with_memory_space_constraint(operand, pltpu.HBM) for operand in operands))


def position():
    member = lax.axis_index("grp")
    group = lax.axis_index("seq")
    return member % 4, member // 4, group % 2, group // 2


def bit(index, level):
    return ((index >> level) & 1).astype(F32)


def query_kernel(width, tok, wq, q_ref):
    pair = 2 * width
    for j in range(wq.shape[1] // pair):
        columns = slice(j * pair, (j + 1) * pair)
        q_ref[:, columns] = unit_pair(dot(tok[...], wq[:, columns]), width)


def query_of(tok, wq, width):
    return pl.pallas_call(
        functools.partial(query_kernel, width),
        out_shape=jax.ShapeDtypeStruct((tok.shape[0], wq.shape[1]), BF16),
        in_specs=[VMEM, VMEM],
        out_specs=VMEM,
        compiler_params=pltpu.CompilerParams(vmem_limit_bytes=12 << 20),
        name="query",
    )(tok, wq)


def inside_kernel(width, first, q_ref, k_ref, v_ref, levels, after, inside_ref):
    rows, columns_here = inside_ref.shape
    block = rows // 2
    low = lax.broadcasted_iota(jnp.int32, (block, block), 0) >= lax.broadcasted_iota(
        jnp.int32, (block, block), 1
    )
    for local in range(columns_here // width):
        head = first + local
        columns = slice(head * width, (head + 1) * width)
        scale = levels[0, head]
        for i in range(2):
            here = slice(i * block, (i + 1) * block)
            q = q_ref[here, columns]

            def weigh(keys, masked):
                scores = lax.dot_general(
                    q, keys, (((1,), (1,)), ((), ())), preferred_element_type=F32
                )
                if masked:
                    scores = jnp.where(low, scores, 0.0)
                return (scores * scale).astype(BF16)

            out = dot(weigh(k_ref[here, columns], True), v_ref[here, columns])
            if i:
                out = out + dot(weigh(k_ref[:block, columns], False), v_ref[:block, columns])
            inside_ref[here, local * width : (local + 1) * width] = out


def inside_of(query, keys, values, level_weights, after, first, count, width):
    return pl.pallas_call(
        functools.partial(inside_kernel, width, first),
        out_shape=jax.ShapeDtypeStruct((query.shape[0], count * width), F32),
        in_specs=[VMEM, VMEM, VMEM, SMEM, ANY],
        out_specs=VMEM,
        compiler_params=pltpu.CompilerParams(vmem_limit_bytes=12 << 20),
        name="inside",
    )(query, keys, values, level_weights, after)


def gather_kernel(levels, *refs):
    near = refs[:4]
    crossed, mine, z1, z2, z3, other2, local_ref, last_ref = refs[4:]
    y, x, core, z = position()
    heads = levels.shape[1]
    part = mine.shape[0] // heads
    for head in range(heads):
        rows = slice(head * part, (head + 1) * part)

        def factor(level, present):
            return levels[level + 1, head] * (present * 2.0 ** (-0.5 * level))

        def read(ref):
            return ref[rows, :].astype(F32)

        far = (
            factor(2, bit(x, 0)) * crossed[0, rows, :].astype(F32)
            + factor(3, bit(x, 1)) * crossed[1, rows, :].astype(F32)
            + factor(4, bit(core ^ 1, 0)) * read(mine)
            + factor(5, bit(z, 0)) * read(z1)
            + factor(6, bit(z, 1)) * (read(z2) + read(z3) + read(other2))
        )
        sides = [read(ref) for ref in near]
        for distance in range(4):
            target = y ^ distance
            local_ref[distance, rows, :] = (
                far
                + factor(0, bit(target, 0)) * sides[distance ^ 1]
                + factor(1, bit(target, 1)) * (sides[distance ^ 2] + sides[distance ^ 3])
            )
        last_ref[rows, :] = jnp.full((part, last_ref.shape[1]), factor(7, bit(z, 2)), F32)


def gather_of(level_weights, near, others):
    shape = near[0].shape
    return pl.pallas_call(
        gather_kernel,
        out_shape=(jax.ShapeDtypeStruct((4, *shape), F32), jax.ShapeDtypeStruct(shape, F32)),
        in_specs=[SMEM] + [VMEM] * 10,
        out_specs=[VMEM, VMEM],
        compiler_params=pltpu.CompilerParams(vmem_limit_bytes=4 << 20),
        name="gather",
    )(level_weights, *near, *others)


def mix_kernel(
    width, q_ref, *refs
):
    insides = refs[:3]
    own, one, two, three, wo, out_hbm, slices, attended, out, sems = refs[3:]
    rows, inner = q_ref.shape
    part = width // QUARTERS
    pair = 2 * width
    y = lax.axis_index("grp") % QUARTERS
    for distance, source in enumerate((own, one, two, three)):
        slices[y ^ distance] = source[...]
    zero = jnp.zeros((width, width), BF16)
    pairs = inner // pair

    def states(j):
        halves = []
        for side in range(2):
            head = 2 * j + side
            state = jnp.concatenate(
                [slices[q, head * part : (head + 1) * part, :] for q in range(QUARTERS)], 0
            )
            halves.append(jnp.concatenate([zero, state] if side else [state, zero], 1))
        return jnp.concatenate(halves, 0)

    blocks = 2
    height = rows // blocks
    steps = sems.shape[0] // blocks
    block = out.shape[1] // steps
    copies = []

    def attend(i):
        here = slice(i * height, (i + 1) * height)
        for j in range(pairs):
            columns = slice(j * pair, (j + 1) * pair)
            attended[here, columns] = (
                insides[j][here, :] + dot(q_ref[here, columns], states(j))
            ).astype(BF16)

    def project(i):
        here = pl.ds(i * height, height)
        for step in range(steps):
            columns = pl.ds(step * block, block)
            out[here, columns] = dot(attended[here, :], wo[:, columns]).astype(BF16)
            copy = pltpu.make_async_copy(
                out.at[here, columns], out_hbm.at[here, columns], sems.at[len(copies)]
            )
            copy.start()
            copies.append(copy)

    attend(0)
    for i in range(blocks):
        if i + 1 < blocks:
            attend(i + 1)
        project(i)
    for copy in copies:
        copy.wait()


def mixed_of(query, insides, pieces, w_output, width):
    rows, inner = query.shape
    wide = w_output.shape[1]
    return pl.pallas_call(
        functools.partial(mix_kernel, width),
        out_shape=jax.ShapeDtypeStruct((rows, wide), BF16),
        in_specs=[VMEM] * 9,
        out_specs=HBM,
        scratch_shapes=[
            pltpu.VMEM((QUARTERS, inner // QUARTERS, width), BF16),
            pltpu.VMEM((rows, inner), BF16),
            pltpu.VMEM((rows, wide), BF16),
            pltpu.SemaphoreType.DMA((6,)),
        ],
        compiler_params=pltpu.CompilerParams(vmem_limit_bytes=16 << 20),
        name="mix",
    )(query, *insides, *pieces, w_output)


AXES = ("seq", "grp")
CORE, Y, X, Z = 16, 1, 4, 32


def flip(value, mask):
    devices = lax.axis_size("seq") * lax.axis_size("grp")
    return lax.ppermute(value, AXES, [(source, source ^ mask) for source in range(devices)])


def plus(total, others):
    for other in others:
        total = total + other.astype(F32)
    return total


def per_device(tokens, w_query, w_key, w_value, w_output, level_weights):
    heads = level_weights.shape[1]
    width = w_query.shape[1] // heads
    keys, values, tok, wq, *sent = states_of(tokens, w_key, w_value, w_query, heads, width)
    n2, n3, n1, n0 = (
        flip(sent[2], CORE | 2 * Y),
        flip(sent[3], CORE | 3 * Y),
        flip(sent[1], CORE | Y),
        flip(sent[0], CORE),
    )
    query = query_of(tok, wq, width)
    n2, n3, n1, n0, query = lax.optimization_barrier((n2, n3, n1, n0, query))
    near = (n0, n1, n2, n3)
    going = plus(n0.astype(F32), near[1:]).astype(BF16)

    x2, x3, x1 = (flip(going, CORE | distance * X) for distance in (2, 3, 1))
    own = flip(going, CORE)
    inside0 = inside_of(query, keys, values, level_weights, going, 0, 2, width)
    x2, x3, x1, own, inside0 = lax.optimization_barrier((x2, x3, x1, own, inside0))
    total = plus(own.astype(F32), (x1, x2, x3))
    mine = total.astype(BF16)

    other = flip(mine, CORE)
    z2 = flip(mine, CORE | 2 * Z)
    total = plus(total, (other,))
    going = total.astype(BF16)
    z3, z1 = flip(going, CORE | 3 * Z), flip(going, CORE | Z)
    other2 = flip(z2, CORE)
    inside1 = inside_of(query, keys, values, level_weights, going, 2, 2, width)
    crossing = jnp.stack([x1.astype(F32), plus(x2.astype(F32), (x3,))]).astype(BF16)
    crossing, inside1 = lax.optimization_barrier((crossing, inside1))
    crossed = flip(crossing, CORE)
    other2, z3, z1, inside1 = lax.optimization_barrier((other2, z3, z1, inside1))
    going = plus(total, (z2, z3, z1, other2)).astype(BF16)

    past = flip(going, CORE | 6 * Z)
    gathered, factor = gather_of(level_weights, near, (crossed, mine, z1, z2, z3, other2))
    past, gathered, factor = lax.optimization_barrier((past, gathered, factor))
    last = factor * past.astype(F32)
    back = [(gathered[distance] + last).astype(BF16) for distance in range(4)]
    p2, p3, p1, p0 = (
        flip(back[2], CORE | 2 * Y),
        flip(back[3], CORE | 3 * Y),
        flip(back[1], CORE | Y),
        flip(back[0], CORE),
    )
    inside2 = inside_of(query, keys, values, level_weights, back[0], 4, 2, width)
    p2, p3, p1, p0, inside2 = lax.optimization_barrier((p2, p3, p1, p0, inside2))
    return mixed_of(query, (inside0, inside1, inside2), (p0, p1, p2, p3), w_output, width)


def solution(mesh):
    placed = (P(("seq", "grp"), None), P(), P(), P(), P(), P())
    return jax.shard_map(
        per_device, mesh=mesh, in_specs=placed, out_specs=P(("seq", "grp"), None), check_vma=False
    )
```
